512 devices in a mesh: gx: 32 (over y, x, core), gy: 16 (over z).
Axes of the slice: x: 4, y: 4, z: 16, core: 2. Of those that a mesh axis runs over, the one named last changes fastest.
Arguments:
- start: float32 [64, 16, 1024], P('gx', 'gy'), may hold values from -6 to 6
- source: float32 [64, 16, 1024], P('gx', 'gy'), may hold values from -4 to 4
- diag_inverse: bfloat16 [64, 16, 16, 4096], P('gx', 'gy'), may hold values from -0.75 to 0.75
- x_lower: bfloat16 [64, 16, 16, 4096], P('gx', 'gy'), may hold values from -1 to 1
- x_upper: bfloat16 [64, 16, 16, 4096], P('gx', 'gy'), may hold values from -1 to 1
- side_blocks: bfloat16 [4, 64, 16, 16, 4096], P(None, 'gx', 'gy'), may hold values from -0.25 to 0.25
Outputs:
- forward: float32 [64, 16, 1024], P('gx', 'gy')
- result: float32 [64, 16, 1024], P('gx', 'gy')
The draws below stay inside these ranges and needn't reach their ends.
All inputs are finite; a program needn't handle non-finite values.
Results may differ from the reference program's by a relative error of at most 0.0003.
Values sent between devices are 32-bit elements; how exact they have to be, the bound alone decides.
A program may use at most 64 MiB of HBM per device.

```python
import math
import jax
import jax.numpy as jnp
from jax import lax

S = 64
NZ = 16
CELLS_FIRST_AXIS = 64
NY = 16


def coupling(key, salt):
    key = jax.random.fold_in(key, salt)
    random_keys = jax.random.split(key, 6)
    order = jax.random.permutation(random_keys[0], S)
    share = S // 2
    slow = order < share
    decay = jnp.exp(jax.random.uniform(random_keys[1], (CELLS_FIRST_AXIS, NY, NZ, S), jnp.float32, math.log(0.7), math.log(2.3)))
    gentle_reaction_rate = jnp.exp(-decay / CELLS_FIRST_AXIS)
    sudden_pulse = jax.random.bernoulli(random_keys[2], 3.0 / CELLS_FIRST_AXIS, (CELLS_FIRST_AXIS, 1, 1, 1))
    residual_error = jax.random.uniform(random_keys[3], (CELLS_FIRST_AXIS, 1, 1, 1), jnp.float32, 0.5, 0.8)
    gentle_reaction_rate = gentle_reaction_rate * jnp.where(sudden_pulse, residual_error, 1.0)
    fast_rate = jax.random.uniform(random_keys[4], (CELLS_FIRST_AXIS, NY, NZ, S), jnp.float32, 0.1, 0.5)
    rate = jnp.where(slow, gentle_reaction_rate, fast_rate)
    noise = jnp.clip(jax.random.normal(random_keys[5], (CELLS_FIRST_AXIS, NY, NZ, S, S), jnp.float32), -4.0, 4.0)
    spread = jnp.where(slow, 0.003, 0.06)[:, None]
    unit_matrix = jnp.eye(S, dtype=jnp.float32)
    matrix = noise * spread * (1.0 - unit_matrix) + rate[..., None] * unit_matrix
    return (-matrix).reshape(CELLS_FIRST_AXIS, NY, NZ, S * S).astype(jnp.bfloat16)


def draw_x_lower(key, part):
    return coupling(key, 11)


def draw_x_upper(key, part):
    return coupling(key, 23)


def steps_of(stream_key, dims, pieces, smallest, largest):
    loudness, own = 1.0, jax.random.fold_in(stream_key, 6)
    for dim, blocks in pieces:
        heights = jnp.exp(jax.random.uniform(jax.random.fold_in(own, dim), (blocks,), jnp.float32, smallest / len(pieces), largest / len(pieces)))
        loudness = loudness * jnp.repeat(heights, dims[dim] // blocks).reshape([-1 if axis == dim else 1 for axis in range(len(dims))])
    return loudness


def centred(stream_key, dims, scale, bound, pieces=(), kind=jnp.bfloat16):
    gain = steps_of(stream_key, dims, pieces, -0.22, 0.18) if pieces else 1.0
    values = jax.random.normal(stream_key, dims, jnp.float32) * scale * gain
    return jnp.minimum(jnp.maximum(values, -bound), bound).astype(kind)


def setup_inputs(seed: int = 0) -> dict:
    splits = jax.random.split(jax.random.key(seed), 7)
    start = centred(splits[0], (CELLS_FIRST_AXIS, NY, NZ * S), 0.5, 6.0, ((0, 32), (1, 16)), jnp.float32)
    source = centred(splits[1], (CELLS_FIRST_AXIS, NY, NZ * S), 0.25, 4.0, ((0, 32), (1, 16)), jnp.float32)
    diag_inverse = centred(splits[2], (CELLS_FIRST_AXIS, NY, NZ, S * S), S ** -0.5, 0.75, ((0, 32), (1, 16)))
    x_lower = draw_x_lower(jax.random.fold_in(splits[6], 71), 0)
    x_upper = draw_x_upper(jax.random.fold_in(splits[6], 71), 0)
    side_blocks = centred(splits[5], (4, CELLS_FIRST_AXIS, NY, NZ, S * S), (8 * S) ** -0.5, 0.25, ((1, 32), (2, 16)))
    return dict(start=start, source=source, diag_inverse=diag_inverse, x_lower=x_lower, x_upper=x_upper, side_blocks=side_blocks)


def apply_block(block, column_values):
    lead = column_values.shape[:-1]
    depth = block.shape[-2]
    width = column_values.shape[-1] // depth
    matrix = block.astype(jnp.float32).reshape(lead + (depth, width, width))
    column = column_values.reshape(lead + (depth, width))
    product = jnp.einsum("...zab,...zb->...za", matrix, column, precision=lax.Precision.HIGHEST)
    return product.reshape(lead + (depth * width,))


def z_terms(side_blocks, column_values, depth):
    width = column_values.shape[-1] // depth
    cells = column_values.reshape(column_values.shape[:-1] + (depth, width))
    zero = jnp.zeros_like(cells[..., :1, :])
    below = jnp.concatenate([zero, cells[..., :-1, :]], -2).reshape(column_values.shape)
    above = jnp.concatenate([cells[..., 1:, :], zero], -2).reshape(column_values.shape)
    return apply_block(side_blocks[2], below) + apply_block(side_blocks[3], above)


def reference(start, source, diag_inverse, x_lower, x_upper, side_blocks):
    depth = NZ
    rhs = apply_block(diag_inverse, source)

    def sideways_coupling(column_values):
        padded = jnp.pad(column_values, ((0, 0), (1, 1), (0, 0)))
        total = apply_block(side_blocks[0], padded[:, :-2]) + apply_block(side_blocks[1], padded[:, 2:])
        return total + z_terms(side_blocks, column_values, depth)

    ahead = jnp.concatenate([start[1:], jnp.zeros_like(start[:1])], 0)
    drive_f = rhs - sideways_coupling(start) - apply_block(x_upper, ahead)

    def advance(previous, inputs):
        drive, block = inputs
        fresh = drive - apply_block(block, previous)
        return fresh, fresh

    initial = jnp.zeros(start.shape[1:], jnp.float32)
    _, forward = lax.scan(advance, initial, (drive_f, x_lower))
    behind = jnp.concatenate([jnp.zeros_like(forward[:1]), forward[:-1]], 0)
    drive_b = rhs - sideways_coupling(forward) - apply_block(x_lower, behind)
    _, reverse_out = lax.scan(advance, initial, (drive_b[::-1], x_upper[::-1]))
    result = reverse_out[::-1]
    return forward, result
```

```python
import functools

import jax
import jax.numpy as jnp
from jax import lax
from jax.experimental import pallas as pl
from jax.experimental.pallas import tpu as pltpu
from jax.sharding import PartitionSpec as P

MESH = pl.DeviceIdType.MESH
F32 = jnp.float32
BF16 = jnp.bfloat16
CHUNK = 8


def lane_of(shape):
    return lax.broadcasted_iota(jnp.int32, shape, len(shape) - 1)


def row_of(shape):
    return lax.broadcasted_iota(jnp.int32, shape, len(shape) - 2)


def swap_halves(x):
    return pltpu.roll(x, 64, 1)


def kernel(nx, ny, nz, *refs):
    (start, source, diag, lower, upper, side, forward_out, result_out,
     v_start, v_source, v_diag, v_lower, v_upper, v_side,
     halo_dn, halo_up, ahead, pad, spread, cells, m_f, m_b, m_in, b_f, b_b, b_in, state, e_f, e_b,
     f_mine, f_dn, f_up,
     load_sem, halo_send, halo_recv, m_send, m_recv, b_send, b_recv, e_send, e_recv, f_send, f_recv) = refs
    me, my = lax.axis_index("gx"), lax.axis_index("gy")
    core, chip = lax.rem(me, 2), lax.div(me, 2)
    low, high, before = my > 0, my < ny - 1, me > 0
    last = me == nx - 1

    barrier = pltpu.get_barrier_semaphore()

    @pl.when(low)
    def _():
        pl.semaphore_signal(barrier, inc=1, device_id=(me, my - 1), device_id_type=MESH)

    @pl.when(high)
    def _():
        pl.semaphore_signal(barrier, inc=1, device_id=(me, my + 1), device_id_type=MESH)

    def greet(i, carry):
        pl.semaphore_signal(barrier, inc=1, device_id=(lax.rem(me + i, nx), my), device_id_type=MESH)
        return carry

    lax.fori_loop(1, nx, greet, 0)

    loads = [pltpu.make_async_copy(a, b, load_sem.at[i]) for i, (a, b) in enumerate(
        ((start, v_start), (lower, v_lower), (source, v_source), (diag, v_diag), (side, v_side), (upper, v_upper)))]
    for load in loads:
        load.start()

    def widen(x, top):
        lanes = lane_of(x.shape)
        turned = swap_halves(x)
        spread[pl.ds(top, 8 * nz // 16, stride=2), :] = jnp.where(lanes < 64, x, turned)
        spread[pl.ds(top + 1, 8 * nz // 16, stride=2), :] = jnp.where(lanes < 64, turned, x)
        return spread[top:top + nz, :]

    def narrow(x):
        spread[0:nz, :] = x
        even = spread[pl.ds(0, nz // 2, stride=2), :]
        odd = spread[pl.ds(1, nz // 2, stride=2), :]
        return jnp.where(lane_of(even.shape) < 64, even, odd)

    def shifted(x):
        pad[8:8 + nz, :] = x
        return pad[7:7 + nz, :], pad[9:9 + nz, :]

    pad[...] = jnp.zeros_like(pad)

    pick = jnp.where(lax.div(lax.rem(row_of((256, 128)), 128), 64) == lax.rem(lane_of((256, 128)), 2), 1.0, 0.0).astype(BF16)

    def apply(terms):
        out = jnp.zeros((nz, 128), F32)
        lanes = lax.div(lax.rem(lane_of((nz, 128)), 64), 2)
        for base in range(0, 32, CHUNK):
            pieces = []
            for c in range(base, base + CHUNK):
                total = None
                for block, vector in terms:
                    term = block[:, c * 128:(c + 1) * 128].astype(F32) * vector
                    total = term if total is None else total + term
                pieces.append(total)
            flat = jnp.concatenate(pieces, axis=0)
            high_part = flat.astype(BF16)
            low_part = (flat - high_part.astype(F32)).astype(BF16)
            sums = jnp.dot(jnp.concatenate([high_part, low_part], axis=1), pick, preferred_element_type=F32)
            for i in range(CHUNK):
                out = jnp.where(lanes == base + i, sums[i * nz:(i + 1) * nz, :], out)
        return out

    def square(z, slot):
        return cells[pl.ds(slot * 32 * nz + z, 32, stride=nz), :]

    def lay_out(block, slot, by=None):
        for c in range(32):
            piece = block[:, c * 128:(c + 1) * 128]
            piece = piece.astype(F32) if by is None else jnp.dot(piece, by, preferred_element_type=F32)
            cells[slot * 32 * nz + c * nz:slot * 32 * nz + (c + 1) * nz, :] = piece

    source_lane = row_of((128, 128))
    target = lax.div(source_lane, 64) * 64 + lax.rem(source_lane, 2) * 32 + lax.div(lax.rem(source_lane, 64), 2)
    sort = jnp.where(target == lane_of((128, 128)), 1.0, 0.0).astype(BF16)

    def compose(later, earlier, out):
        lay_out(later, 0, sort)
        lay_out(earlier, 1)
        lanes = lane_of((32, 128))
        for z in range(nz):
            b = square(z, 1)
            turned = swap_halves(b)
            right = jnp.concatenate([
                jnp.where(lanes < 64, b, 0.0), jnp.where(lanes < 64, turned, 0.0),
                jnp.where(lanes < 64, 0.0, turned), jnp.where(lanes < 64, 0.0, b)], axis=0).astype(BF16)
            out[z] = jnp.dot(square(z, 0).astype(BF16), right, preferred_element_type=F32)

    def compose_both(later, earlier, out, flip):
        @pl.when(jnp.logical_not(flip))
        def _():
            compose(later, earlier, out)

        @pl.when(flip)
        def _():
            compose_turned(later, earlier, out)

    order = jnp.where(lax.div(lane_of((64, 64)), 2) + 32 * lax.rem(lane_of((64, 64)), 2) == row_of((64, 64)), 1.0, 0.0).astype(BF16)

    unorder = jnp.where(lax.div(row_of((64, 64)), 2) + 32 * lax.rem(row_of((64, 64)), 2) == lane_of((64, 64)), 1.0, 0.0).astype(BF16)

    def compose_turned(later, earlier, out):
        lay_out(later, 0, sort)
        lay_out(earlier, 1)
        nt = (((1,), (1,)), ((), ()))
        for z in range(nz):
            a, b = square(z, 0), square(z, 1)
            a_stack = jnp.concatenate([a[:, :64], swap_halves(a)[:, :64]], axis=0).astype(BF16)
            b_stack = jnp.concatenate([b[:, :64], swap_halves(b)[:, :64]], axis=0).astype(BF16)
            b_turned = lax.dot_general(order, b_stack, nt, preferred_element_type=F32).astype(BF16)
            a_rows = jnp.dot(unorder, a_stack, preferred_element_type=F32).astype(BF16)
            turned = lax.dot_general(b_turned, a_rows, nt, preferred_element_type=F32)
            out[z] = jnp.concatenate([turned[:32], turned[32:]], axis=1)

    loads[1].wait()
    compose_both(v_lower.at[1], v_lower.at[0], m_f, core == 1)
    loads[0].wait()
    pl.semaphore_wait(barrier, nx - 1 + low.astype(jnp.int32) + high.astype(jnp.int32))

    def copy(src, dst, send, recv, where):
        return pltpu.make_async_remote_copy(src_ref=src, dst_ref=dst, send_sem=send, recv_sem=recv,
                                            device_id=where, device_id_type=MESH)

    @pl.when(low)
    def _():
        copy(v_start, halo_up, halo_send.at[0], halo_recv.at[0], (me, my - 1)).start()

    @pl.when(high)
    def _():
        copy(v_start, halo_dn, halo_send.at[1], halo_recv.at[1], (me, my + 1)).start()

    @pl.when(before)
    def _():
        copy(v_start.at[0], ahead, halo_send.at[2], halo_recv.at[2], (me - 1, my)).start()

    def to_owners(rows, inbox, slot, side_core, index, send, recv):
        def one(i, carry):
            z = lax.rem(chip + i, nz)
            owner = 2 * z + side_core

            @pl.when(owner != me)
            def _():
                copy(rows.at[z], inbox.at[slot], send.at[index], recv.at[index], (owner, my)).start()

            @pl.when(owner == me)
            def _():
                pltpu.make_async_copy(rows.at[z], inbox.at[slot], recv.at[index]).start()

            return carry

        lax.fori_loop(0, nz, one, 0)

    def from_owner(boxes, side_core, index):
        def one(step, carry):
            to = step if side_core == 0 else nx - 1 - step

            @pl.when(to != me)
            def _():
                copy(state.at[step], boxes.at[chip], e_send, e_recv.at[index], (to, my)).start()

            @pl.when(to == me)
            def _():
                pltpu.make_async_copy(state.at[step], boxes.at[chip], e_recv.at[index]).start()

            return carry

        lax.fori_loop(0, nx, one, 0)

    def landed(ref, sem):
        pltpu.make_async_copy(ref, ref, sem).wait()

    slot_f, slot_b = me, nx - 1 - me
    to_owners(m_f, m_in, slot_f, 0, 0, m_send, m_recv)

    loads[2].wait()
    loads[3].wait()
    loads[4].wait()
    loads[5].wait()
    mine = [widen(v_start[p], 0) for p in range(2)]
    rhs = [apply([(v_diag.at[p], widen(v_source[p], 0))]) for p in range(2)]
    compose_both(v_upper.at[0], v_upper.at[1], m_b, core == 0)

    @pl.when(jnp.logical_not(low))
    def _():
        halo_dn[...] = jnp.zeros_like(halo_dn)

    @pl.when(jnp.logical_not(high))
    def _():
        halo_up[...] = jnp.zeros_like(halo_up)

    @pl.when(last)
    def _():
        ahead[...] = jnp.zeros_like(ahead)

    @pl.when(high)
    def _():
        landed(halo_up, halo_recv.at[0])

    @pl.when(low)
    def _():
        landed(halo_dn, halo_recv.at[1])

    @pl.when(jnp.logical_not(last))
    def _():
        landed(ahead, halo_recv.at[2])

    next_plane = [mine[1], widen(ahead[...], 0)]
    fixed, drive = [], []
    for p in range(2):
        below, above = shifted(mine[p])
        fixed.append(apply([(v_side.at[0, p], widen(halo_dn[p], 0)), (v_side.at[1, p], widen(halo_up[p], 0)),
                            (v_side.at[2, p], below), (v_side.at[3, p], above), (v_upper.at[p], next_plane[p])]))
        drive.append(rhs[p] - fixed[p])

    def put(rows, value):
        for z in range(nz):
            rows[z] = value[z:z + 1, :]

    def take(boxes, which):
        return jnp.concatenate([boxes[z, which] for z in range(nz)], axis=0)

    put(b_f, drive[1] - apply([(v_lower.at[1], drive[0])]))
    to_owners(b_f, b_in, slot_f, 0, 0, b_send, b_recv)
    to_owners(m_b, m_in, slot_b, 1, 1, m_send, m_recv)

    def chain(boxes, side_core):
        index = side_core
        landed(m_in, m_recv.at[index])
        landed(b_in, b_recv.at[index])
        lanes = lane_of((32, 128))
        rows = row_of((32, 128))
        left = lanes < 64
        even_place = lax.rem(lanes, 64) == 2 * rows
        odd_place = lax.rem(lanes, 64) == 2 * rows + 1

        def pair(j, x):
            a, b = m_in[2 * j], jnp.broadcast_to(b_in[2 * j], (32, 128))
            x_rows = jnp.broadcast_to(x, (32, 128))
            even = jnp.sum(jnp.where(left, a * x_rows, 0.0) + jnp.where(jnp.logical_and(left, even_place), b, 0.0),
                           axis=1, keepdims=True)
            odd = jnp.sum(jnp.where(left, 0.0, a * x_rows) + jnp.where(jnp.logical_and(left, odd_place), b, 0.0),
                          axis=1, keepdims=True)
            even, odd = jnp.broadcast_to(even, (32, 128)), jnp.broadcast_to(odd, (32, 128))
            middle = jnp.sum(jnp.where(even_place, even, jnp.where(odd_place, odd, 0.0)), axis=0, keepdims=True)
            state[2 * j, 1] = middle
            state[2 * j + 1, 0] = middle
            t = jnp.sum(m_in[2 * j + 1] * jnp.where(left, even, odd), axis=0, keepdims=True)
            y = t + swap_halves(t) + b_in[2 * j + 1]
            state[2 * j, 0] = x
            state[2 * j + 1, 1] = y
            return y

        zero = jnp.zeros((1, 128), F32)
        lax.fori_loop(0, nx // 2, pair, zero)
        from_owner(boxes, side_core, index)

    @pl.when(core == 0)
    def _():
        chain(e_f, 0)

    landed(e_f, e_recv.at[0])
    f = [drive[0] - apply([(v_lower.at[0], take(e_f, 0))]), take(e_f, 1)]
    for p in range(2):
        f_mine[p] = f[p]

    @pl.when(low)
    def _():
        copy(f_mine, f_up, f_send.at[0], f_recv.at[0], (me, my - 1)).start()

    @pl.when(high)
    def _():
        copy(f_mine, f_dn, f_send.at[1], f_recv.at[1], (me, my + 1)).start()

    @pl.when(jnp.logical_not(low))
    def _():
        f_dn[...] = jnp.zeros_like(f_dn)

    @pl.when(jnp.logical_not(high))
    def _():
        f_up[...] = jnp.zeros_like(f_up)

    partial = []
    for p in range(2):
        forward_out[p] = narrow(f[p])
        below, above = shifted(f[p])
        partial.append(fixed[p] + f[p] - apply([(v_side.at[2, p], below), (v_side.at[3, p], above)]))

    @pl.when(high)
    def _():
        landed(f_up, f_recv.at[0])

    @pl.when(low)
    def _():
        landed(f_dn, f_recv.at[1])

    g = [partial[p] - apply([(v_side.at[0, p], f_dn[p]), (v_side.at[1, p], f_up[p])]) for p in range(2)]
    put(b_b, g[0] - apply([(v_upper.at[0], g[1])]))
    to_owners(b_b, b_in, slot_b, 1, 1, b_send, b_recv)

    @pl.when(core == 1)
    def _():
        chain(e_b, 1)

    landed(e_b, e_recv.at[1])
    result_out[0] = narrow(take(e_b, 1))
    result_out[1] = narrow(g[1] - apply([(v_upper.at[1], take(e_b, 0))]))

    @pl.when(low)
    def _():
        landed(v_start, halo_send.at[0])
        landed(f_mine, f_send.at[0])

    @pl.when(high)
    def _():
        landed(v_start, halo_send.at[1])
        landed(f_mine, f_send.at[1])

    @pl.when(before)
    def _():
        landed(ahead, halo_send.at[2])

    for side_core in range(2):
        for rows, sem in (((m_f, m_b)[side_core], m_send), ((b_f, b_b)[side_core], b_send)):
            @pl.when(core == side_core)
            def _():
                landed(rows.at[pl.ds(0, nz - 1)], sem.at[side_core])

            @pl.when(core != side_core)
            def _():
                landed(rows, sem.at[side_core])

    landed(state.at[pl.ds(0, nx - 1)], e_send)


def solution(mesh):
    nx, ny = mesh.shape["gx"], mesh.shape["gy"]

    def local(start, source, diag, lower, upper, side):
        nz = lower.shape[2]
        half = nz // 2
        width = lower.shape[3]
        any_space = pl.BlockSpec(memory_space=pl.ANY)
        vmem = pl.BlockSpec(memory_space=pltpu.VMEM)
        out = jax.ShapeDtypeStruct((2, half, 128), F32)
        dma = pltpu.SemaphoreType.DMA
        forward, result = pl.pallas_call(
            functools.partial(kernel, nx, ny, nz),
            out_shape=(out, out),
            in_specs=[any_space] * 6,
            out_specs=(vmem, vmem),
            scratch_shapes=[
                pltpu.VMEM((2, half, 128), F32), pltpu.VMEM((2, half, 128), F32),
                pltpu.VMEM((2, nz, width), BF16), pltpu.VMEM((2, nz, width), BF16), pltpu.VMEM((2, nz, width), BF16),
                pltpu.VMEM((4, 2, nz, width), BF16),
                pltpu.VMEM((2, half, 128), F32), pltpu.VMEM((2, half, 128), F32), pltpu.VMEM((half, 128), F32),
                pltpu.VMEM((nz + 16, 128), F32), pltpu.VMEM((nz, 128), F32), pltpu.VMEM((2 * 32 * nz, 128), F32),
                pltpu.VMEM((nz, 32, 128), F32), pltpu.VMEM((nz, 32, 128), F32), pltpu.VMEM((nx, 32, 128), F32),
                pltpu.VMEM((nz, 1, 128), F32), pltpu.VMEM((nz, 1, 128), F32), pltpu.VMEM((nx, 1, 128), F32),
                pltpu.VMEM((nx, 2, 1, 128), F32),
                pltpu.VMEM((nz, 2, 1, 128), F32), pltpu.VMEM((nz, 2, 1, 128), F32),
                pltpu.VMEM((2, nz, 128), F32), pltpu.VMEM((2, nz, 128), F32), pltpu.VMEM((2, nz, 128), F32),
                dma((6,)), dma((3,)), dma((3,)), dma((2,)), dma((2,)), dma((2,)), dma((2,)), dma, dma((2,)),
                dma((2,)), dma((2,)),
            ],
            compiler_params=pltpu.CompilerParams(collective_id=0, has_side_effects=True),
        )(start.reshape(2, half, 128), source.reshape(2, half, 128), diag.reshape(2, nz, width),
          lower.reshape(2, nz, width), upper.reshape(2, nz, width), side.reshape(4, 2, nz, width))
        return forward.reshape(start.shape), result.reshape(start.shape)

    return jax.shard_map(
        local,
        mesh=mesh,
        in_specs=(P("gx", "gy", None), P("gx", "gy", None), P("gx", "gy", None, None), P("gx", "gy", None, None),
                  P("gx", "gy", None, None), P(None, "gx", "gy", None, None)),
        out_specs=(P("gx", "gy", None), P("gx", "gy", None)),
        check_vma=False,
    )
```

```python
import functools

import jax
import jax.numpy as jnp
from jax import lax
from jax.experimental import pallas as pl
from jax.experimental.pallas import tpu as pltpu
from jax.sharding import PartitionSpec as P

MESH = pl.DeviceIdType.MESH
F32 = jnp.float32
BF16 = jnp.bfloat16
CHUNK = 8


def lane_of(shape):
    return lax.broadcasted_iota(jnp.int32, shape, len(shape) - 1)


def row_of(shape):
    return lax.broadcasted_iota(jnp.int32, shape, len(shape) - 2)


def swap_halves(x):
    return pltpu.roll(x, 64, 1)


def kernel(nx, ny, nz, *refs):
    (start, source, diag, lower, upper, side, forward_out, result_out,
     v_start, v_source, v_diag, v_lower, v_upper, v_side,
     halo_dn, halo_up, ahead, pad, spread, cells, m_f, m_b, m_in, b_f, b_b, b_in, state, e_f, e_b, m_odd,
     f_mine, f_dn, f_up,
     load_sem, halo_send, halo_recv, m_send, m_recv, b_send, b_recv, e_send, e_recv, f_send, f_recv,
     hello) = refs
    me, my = lax.axis_index("gx"), lax.axis_index("gy")
    core, chip = lax.rem(me, 2), lax.div(me, 2)
    low, high, before = my > 0, my < ny - 1, me > 0
    edge = 4 if nz == 16 else 2

    def opposite(place):
        half = edge // 2
        return lax.rem(lax.div(place, edge) + half, edge) * edge + lax.rem(lax.rem(place, edge) + half, edge)

    line = jnp.where(core == 0, chip, opposite(chip))
    last = me == nx - 1

    barrier = pltpu.get_barrier_semaphore()

    @pl.when(low)
    def _():
        pl.semaphore_signal(barrier, inc=1, device_id=(me, my - 1), device_id_type=MESH)

    @pl.when(high)
    def _():
        pl.semaphore_signal(barrier, inc=1, device_id=(me, my + 1), device_id_type=MESH)

    def greet(semaphore):
        def one(i, carry):
            pl.semaphore_signal(semaphore, inc=1, device_id=(lax.rem(me + i, nx), my), device_id_type=MESH)
            return carry

        lax.fori_loop(1, nx, one, 0)

    @pl.when(before)
    def _():
        greet(barrier)

    loads = [pltpu.make_async_copy(a, b, load_sem.at[i]) for i, (a, b) in enumerate(
        ((start, v_start), (lower, v_lower), (source, v_source), (diag, v_diag), (side, v_side), (upper, v_upper)))]
    for load in loads:
        load.start()

    def widen(x, top):
        lanes = lane_of(x.shape)
        turned = swap_halves(x)
        spread[pl.ds(top, 8 * nz // 16, stride=2), :] = jnp.where(lanes < 64, x, turned)
        spread[pl.ds(top + 1, 8 * nz // 16, stride=2), :] = jnp.where(lanes < 64, turned, x)
        return spread[top:top + nz, :]

    def narrow(x):
        spread[0:nz, :] = x
        even = spread[pl.ds(0, nz // 2, stride=2), :]
        odd = spread[pl.ds(1, nz // 2, stride=2), :]
        return jnp.where(lane_of(even.shape) < 64, even, odd)

    def shifted(x):
        pad[8:8 + nz, :] = x
        return pad[7:7 + nz, :], pad[9:9 + nz, :]

    pad[...] = jnp.zeros_like(pad)

    pick = jnp.where(lax.div(lax.rem(row_of((256, 128)), 128), 64) == lax.rem(lane_of((256, 128)), 2), 1.0, 0.0).astype(BF16)

    def apply(terms):
        out = jnp.zeros((nz, 128), F32)
        lanes = lax.div(lax.rem(lane_of((nz, 128)), 64), 2)
        for base in range(0, 32, CHUNK):
            pieces = []
            for c in range(base, base + CHUNK):
                total = None
                for block, vector in terms:
                    term = block[:, c * 128:(c + 1) * 128].astype(F32) * vector
                    total = term if total is None else total + term
                pieces.append(total)
            flat = jnp.concatenate(pieces, axis=0)
            high_part = flat.astype(BF16)
            low_part = (flat - high_part.astype(F32)).astype(BF16)
            sums = jnp.dot(jnp.concatenate([high_part, low_part], axis=1), pick, preferred_element_type=F32)
            for i in range(CHUNK):
                out = jnp.where(lanes == base + i, sums[i * nz:(i + 1) * nz, :], out)
        return out

    def square(z, slot):
        return cells[pl.ds(slot * 32 * nz + z, 32, stride=nz), :]

    def lay_out(block, slot, by=None):
        for c in range(32):
            piece = block[:, c * 128:(c + 1) * 128]
            piece = piece.astype(F32) if by is None else jnp.dot(piece, by, preferred_element_type=F32)
            cells[slot * 32 * nz + c * nz:slot * 32 * nz + (c + 1) * nz, :] = piece

    source_lane = row_of((128, 128))
    target = lax.div(source_lane, 64) * 64 + lax.rem(source_lane, 2) * 32 + lax.div(lax.rem(source_lane, 64), 2)
    sort = jnp.where(target == lane_of((128, 128)), 1.0, 0.0).astype(BF16)

    def compose(later, earlier, out):
        lay_out(later, 0, sort)
        lay_out(earlier, 1)
        lanes = lane_of((32, 128))
        for z in range(nz):
            b = square(z, 1)
            turned = swap_halves(b)
            right = jnp.concatenate([
                jnp.where(lanes < 64, b, 0.0), jnp.where(lanes < 64, turned, 0.0),
                jnp.where(lanes < 64, 0.0, turned), jnp.where(lanes < 64, 0.0, b)], axis=0).astype(BF16)
            out[z] = jnp.dot(square(z, 0).astype(BF16), right, preferred_element_type=F32)

    def compose_both(later, earlier, out, flip):
        @pl.when(jnp.logical_not(flip))
        def _():
            compose(later, earlier, out)

        @pl.when(flip)
        def _():
            compose_turned(later, earlier, out)

    order = jnp.where(lax.div(lane_of((64, 64)), 2) + 32 * lax.rem(lane_of((64, 64)), 2) == row_of((64, 64)), 1.0, 0.0).astype(BF16)

    unorder = jnp.where(lax.div(row_of((64, 64)), 2) + 32 * lax.rem(row_of((64, 64)), 2) == lane_of((64, 64)), 1.0, 0.0).astype(BF16)

    def compose_turned(later, earlier, out):
        lay_out(later, 0, sort)
        lay_out(earlier, 1)
        nt = (((1,), (1,)), ((), ()))
        for z in range(nz):
            a, b = square(z, 0), square(z, 1)
            a_stack = jnp.concatenate([a[:, :64], swap_halves(a)[:, :64]], axis=0).astype(BF16)
            b_stack = jnp.concatenate([b[:, :64], swap_halves(b)[:, :64]], axis=0).astype(BF16)
            b_turned = lax.dot_general(order, b_stack, nt, preferred_element_type=F32).astype(BF16)
            a_rows = jnp.dot(unorder, a_stack, preferred_element_type=F32).astype(BF16)
            turned = lax.dot_general(b_turned, a_rows, nt, preferred_element_type=F32)
            out[z] = jnp.concatenate([turned[:32], turned[32:]], axis=1)

    @pl.when(before)
    def _():
        loads[1].wait()
        compose_both(v_lower.at[1], v_lower.at[0], m_f, core == 1)

    pl.semaphore_wait(barrier, nx - 2 + low.astype(jnp.int32) + high.astype(jnp.int32) + (me == 0).astype(jnp.int32))

    @pl.when(me == 0)
    def _():
        greet(hello)
        loads[1].wait()

    loads[0].wait()

    def copy(src, dst, send, recv, where):
        return pltpu.make_async_remote_copy(src_ref=src, dst_ref=dst, send_sem=send, recv_sem=recv,
                                            device_id=where, device_id_type=MESH)

    @pl.when(low)
    def _():
        copy(v_start, halo_up, halo_send.at[0], halo_recv.at[0], (me, my - 1)).start()

    @pl.when(high)
    def _():
        copy(v_start, halo_dn, halo_send.at[1], halo_recv.at[1], (me, my + 1)).start()

    @pl.when(me >= 2)
    def _():
        copy(v_start.at[0], ahead, halo_send.at[2], halo_recv.at[2], (me - 1, my)).start()

    def to_owner(rows, index, z, owner, send, recv):
        slot = slots[index]
        inbox = (m_in if rows.shape[1] == 32 else b_in).at[index]

        @pl.when(owner != me)
        def _():
            copy(rows.at[z], inbox.at[slot], send.at[index], recv.at[index], (owner, my)).start()

        @pl.when(owner == me)
        def _():
            pltpu.make_async_copy(rows.at[z], inbox.at[slot], recv.at[index]).start()

    def to_owners(rows, index, send, recv):
        def one(i, carry):
            z = lax.rem(chip + i, nz)
            if index == 0:
                to_owner(rows, index, z, 2 * z + 1, send, recv)
            else:
                to_owner(rows, index, z, 2 * z, send, recv)
                to_owner(rows, index, z, 2 * opposite(z) + 1, send, recv)
            return carry

        lax.fori_loop(0, nz, one, 0)

    def from_owner(boxes, index):
        half = edge // 2
        near = []
        for ry in range(edge):
            for rx in range(edge):
                hops = min(rx, edge - rx) + min(ry, edge - ry)
                if index == 0 or hops < half or (hops == half and 1 <= rx <= half):
                    near.append((-hops, ry, rx))
        for hops, ry, rx in sorted(near):
            there = lax.rem(lax.div(chip, edge) + ry, edge) * edge + lax.rem(lax.rem(chip, edge) + rx, edge)
            for which in range(2):
                to = 2 * there + which
                step = to if index == 0 else nx - 1 - to
                src, dst = state.at[index, step], boxes.at[chip if index == 0 else line]
                if hops:
                    copy(src, dst, e_send.at[index], e_recv.at[index], (to, my)).start()
                else:
                    @pl.when(core != which)
                    def _():
                        copy(src, dst, e_send.at[index], e_recv.at[index], (to, my)).start()

                    @pl.when(core == which)
                    def _():
                        pltpu.make_async_copy(src, dst, e_recv.at[index]).start()

    def landed(ref, sem):
        pltpu.make_async_copy(ref, ref, sem).wait()

    slots = (me, nx - 1 - me)

    @pl.when(before)
    def _():
        to_owners(m_f, 0, m_send, m_recv)

    @pl.when(me == 1)
    def _():
        pl.semaphore_wait(hello, 1)
        copy(v_start.at[0], ahead, halo_send.at[2], halo_recv.at[2], (me - 1, my)).start()

    loads[2].wait()
    loads[3].wait()
    loads[4].wait()
    loads[5].wait()
    mine = [widen(v_start[p], 0) for p in range(2)]
    rhs = [apply([(v_diag.at[p], widen(v_source[p], 0))]) for p in range(2)]

    @pl.when(jnp.logical_not(low))
    def _():
        halo_dn[...] = jnp.zeros_like(halo_dn)

    @pl.when(jnp.logical_not(high))
    def _():
        halo_up[...] = jnp.zeros_like(halo_up)

    @pl.when(last)
    def _():
        ahead[...] = jnp.zeros_like(ahead)

    @pl.when(high)
    def _():
        landed(halo_up, halo_recv.at[0])

    @pl.when(low)
    def _():
        landed(halo_dn, halo_recv.at[1])

    @pl.when(jnp.logical_not(last))
    def _():
        landed(ahead, halo_recv.at[2])

    next_plane = [mine[1], widen(ahead[...], 0)]
    fixed, drive = [], []
    for p in range(2):
        below, above = shifted(mine[p])
        fixed.append(apply([(v_side.at[0, p], widen(halo_dn[p], 0)), (v_side.at[1, p], widen(halo_up[p], 0)),
                            (v_side.at[2, p], below), (v_side.at[3, p], above), (v_upper.at[p], next_plane[p])]))
        drive.append(rhs[p] - fixed[p])

    def put(rows, value):
        for z in range(nz):
            rows[z] = value[z:z + 1, :]

    def take(boxes, which):
        return jnp.concatenate([boxes[z, which] for z in range(nz)], axis=0)

    put(b_f, drive[1] - apply([(v_lower.at[1], drive[0])]))
    to_owners(b_f, 0, b_send, b_recv)

    @pl.when(me >= 2)
    def _():
        pl.semaphore_wait(hello, 1)

    compose_both(v_upper.at[0], v_upper.at[1], m_b, core == 0)
    to_owners(m_b, 1, m_send, m_recv)

    def chain(boxes, index):
        if index == 0:
            landed(m_in.at[0, pl.ds(0, nx - 1)], m_recv.at[0])
            m_in[0, 0] = jnp.zeros((32, 128), F32)
        else:
            landed(m_in.at[1], m_recv.at[1])
        lanes = lane_of((32, 128))
        rows = row_of((32, 128))
        left = lanes < 64
        even_place = lax.rem(lanes, 64) == 2 * rows
        odd_place = lax.rem(lanes, 64) == 2 * rows + 1
        left_row = lane_of((1, 128)) < 64

        def double(j, carry):
            a = m_in[index, 2 * j]
            turned = swap_halves(a)
            m_in[index, 2 * j] = jnp.where(left, a, turned)
            m_odd[j] = jnp.where(left, turned, a)
            return carry

        lax.fori_loop(0, nx // 2, double, 0, unroll=4)
        landed(b_in.at[index], b_recv.at[index])

        def pair(j, x):
            b = jnp.broadcast_to(b_in[index, 2 * j], (32, 128))
            x_rows = jnp.broadcast_to(x, (32, 128))
            even = jnp.sum(m_in[index, 2 * j] * x_rows
                           + jnp.where(jnp.logical_and(left, even_place), b, 0.0), axis=1, keepdims=True)
            odd = jnp.sum(m_odd[j] * x_rows
                          + jnp.where(jnp.logical_and(left, odd_place), b, 0.0), axis=1, keepdims=True)
            even, odd = jnp.broadcast_to(even, (32, 128)), jnp.broadcast_to(odd, (32, 128))
            y = (jnp.sum(m_in[index, 2 * j + 1] * jnp.where(left, even, odd), axis=0, keepdims=True)
                 + jnp.where(left_row, b_in[index, 2 * j + 1], 0.0))
            middle = jnp.sum(jnp.where(even_place, even, jnp.where(odd_place, odd, 0.0)), axis=0, keepdims=True)
            state[index, 2 * j, 0] = x + swap_halves(x)
            state[index, 2 * j, 1] = middle
            state[index, 2 * j + 1, 0] = middle
            state[index, 2 * j + 1, 1] = y + swap_halves(y)
            return y

        lax.fori_loop(0, nx // 2, pair, jnp.zeros((1, 128), F32), unroll=True)
        from_owner(boxes, index)

    @pl.when(core == 1)
    def _():
        chain(e_f, 0)

    landed(e_f, e_recv.at[0])
    f = [drive[0] - apply([(v_lower.at[0], take(e_f, 0))]), take(e_f, 1)]
    for p in range(2):
        f_mine[p] = f[p]

    @pl.when(low)
    def _():
        copy(f_mine, f_up, f_send.at[0], f_recv.at[0], (me, my - 1)).start()

    @pl.when(high)
    def _():
        copy(f_mine, f_dn, f_send.at[1], f_recv.at[1], (me, my + 1)).start()

    @pl.when(jnp.logical_not(low))
    def _():
        f_dn[...] = jnp.zeros_like(f_dn)

    @pl.when(jnp.logical_not(high))
    def _():
        f_up[...] = jnp.zeros_like(f_up)

    partial = []
    for p in range(2):
        forward_out[p] = narrow(f[p])
        below, above = shifted(f[p])
        partial.append(fixed[p] + f[p] - apply([(v_side.at[2, p], below), (v_side.at[3, p], above)]))

    @pl.when(high)
    def _():
        landed(f_up, f_recv.at[0])

    @pl.when(low)
    def _():
        landed(f_dn, f_recv.at[1])

    g = [partial[p] - apply([(v_side.at[0, p], f_dn[p]), (v_side.at[1, p], f_up[p])]) for p in range(2)]
    put(b_b, g[0] - apply([(v_upper.at[0], g[1])]))
    to_owners(b_b, 1, b_send, b_recv)
    chain(e_b, 1)

    landed(e_b, e_recv.at[1])
    result_out[0] = narrow(take(e_b, 1))
    result_out[1] = narrow(g[1] - apply([(v_upper.at[1], take(e_b, 0))]))

    @pl.when(low)
    def _():
        landed(v_start, halo_send.at[0])
        landed(f_mine, f_send.at[0])

    @pl.when(high)
    def _():
        landed(v_start, halo_send.at[1])
        landed(f_mine, f_send.at[1])

    @pl.when(before)
    def _():
        landed(ahead, halo_send.at[2])

    @pl.when(core == 1)
    def _():
        landed(m_f.at[pl.ds(0, nz - 1)], m_send.at[0])
        landed(b_f.at[pl.ds(0, nz - 1)], b_send.at[0])
        landed(state.at[0, pl.ds(0, nx - 1)], e_send.at[0])

    @pl.when(core == 0)
    def _():
        landed(b_f, b_send.at[0])

    @pl.when(jnp.logical_and(core == 0, before))
    def _():
        landed(m_f, m_send.at[0])

    landed(m_in.at[1, pl.ds(0, nx - 1)], m_send.at[1])
    landed(b_in.at[1, pl.ds(0, nx - 1)], b_send.at[1])
    landed(state.at[1, pl.ds(0, nz - 1)], e_send.at[1])


def hand_out(forward_in, result_in, forward_out, result_out):
    forward_out[...] = forward_in[...]
    result_out[...] = result_in[...]


def solution(mesh):
    nx, ny = mesh.shape["gx"], mesh.shape["gy"]

    def local(start, source, diag, lower, upper, side):
        nz = lower.shape[2]
        half = nz // 2
        width = lower.shape[3]
        any_space = pl.BlockSpec(memory_space=pl.ANY)
        vmem = pl.BlockSpec(memory_space=pltpu.VMEM)
        out = jax.ShapeDtypeStruct((2, half, 128), F32)
        dma = pltpu.SemaphoreType.DMA
        forward, result = pl.pallas_call(
            functools.partial(kernel, nx, ny, nz),
            out_shape=(out, out),
            in_specs=[any_space] * 6,
            out_specs=(vmem, vmem),
            scratch_shapes=[
                pltpu.VMEM((2, half, 128), F32), pltpu.VMEM((2, half, 128), F32),
                pltpu.VMEM((2, nz, width), BF16), pltpu.VMEM((2, nz, width), BF16), pltpu.VMEM((2, nz, width), BF16),
                pltpu.VMEM((4, 2, nz, width), BF16),
                pltpu.VMEM((2, half, 128), F32), pltpu.VMEM((2, half, 128), F32), pltpu.VMEM((half, 128), F32),
                pltpu.VMEM((nz + 16, 128), F32), pltpu.VMEM((nz, 128), F32), pltpu.VMEM((2 * 32 * nz, 128), F32),
                pltpu.VMEM((nz, 32, 128), F32), pltpu.VMEM((nz, 32, 128), F32), pltpu.VMEM((2, nx, 32, 128), F32),
                pltpu.VMEM((nz, 1, 128), F32), pltpu.VMEM((nz, 1, 128), F32), pltpu.VMEM((2, nx, 1, 128), F32),
                pltpu.VMEM((2, nx, 2, 1, 128), F32),
                pltpu.VMEM((nz, 2, 1, 128), F32), pltpu.VMEM((nz, 2, 1, 128), F32), pltpu.VMEM((nx // 2, 32, 128), F32),
                pltpu.VMEM((2, nz, 128), F32), pltpu.VMEM((2, nz, 128), F32), pltpu.VMEM((2, nz, 128), F32),
                dma((6,)), dma((3,)), dma((3,)), dma((2,)), dma((2,)), dma((2,)), dma((2,)), dma((2,)), dma((2,)),
                dma((2,)), dma((2,)), pltpu.SemaphoreType.REGULAR,
            ],
            compiler_params=pltpu.CompilerParams(collective_id=0, has_side_effects=True),
        )(start.reshape(2, half, 128), source.reshape(2, half, 128), diag.reshape(2, nz, width),
          lower.reshape(2, nz, width), upper.reshape(2, nz, width), side.reshape(4, 2, nz, width))
        forward, result = pl.pallas_call(
            hand_out, out_shape=(out, out), in_specs=[vmem, vmem], out_specs=(vmem, vmem))(forward, result)
        return forward.reshape(start.shape), result.reshape(start.shape)

    return jax.shard_map(
        local,
        mesh=mesh,
        in_specs=(P("gx", "gy", None), P("gx", "gy", None), P("gx", "gy", None, None), P("gx", "gy", None, None),
                  P("gx", "gy", None, None), P(None, "gx", "gy", None, None)),
        out_specs=(P("gx", "gy", None), P("gx", "gy", None)),
        check_vma=False,
    )
```

```python
import functools

import jax
import jax.numpy as jnp
from jax import lax
from jax.experimental import pallas as pl
from jax.experimental.pallas import tpu as pltpu
from jax.sharding import PartitionSpec as P

MESH = pl.DeviceIdType.MESH
F32 = jnp.float32
BF16 = jnp.bfloat16
CHUNK = 8


def lane_of(shape):
    return lax.broadcasted_iota(jnp.int32, shape, len(shape) - 1)


def row_of(shape):
    return lax.broadcasted_iota(jnp.int32, shape, len(shape) - 2)


def swap_halves(x):
    return pltpu.roll(x, 64, 1)


def kernel(nx, ny, nz, *refs):
    (start, source, diag, lower, upper, side, forward_out, result_out,
     v_start, v_source, v_diag, v_lower, v_upper, v_side,
     halo_dn, halo_up, ahead, pad, spread, cells, m_f, m_b, m_in, b_f, b_b, b_in, state, e_f, e_b, m_odd,
     f_mine, f_dn, f_up,
     load_sem, halo_send, halo_recv, m_send, m_recv, b_send, b_recv, e_send, e_recv, f_send, f_recv,
     hello) = refs
    me, my = lax.axis_index("gx"), lax.axis_index("gy")
    core, chip = lax.rem(me, 2), lax.div(me, 2)
    low, high, before = my > 0, my < ny - 1, me > 0
    edge = 4 if nz == 16 else 2

    def opposite(place):
        half = edge // 2
        return lax.rem(lax.div(place, edge) + half, edge) * edge + lax.rem(lax.rem(place, edge) + half, edge)

    line = jnp.where(core == 0, chip, opposite(chip))
    last = me == nx - 1

    barrier = pltpu.get_barrier_semaphore()

    @pl.when(low)
    def _():
        pl.semaphore_signal(barrier, inc=1, device_id=(me, my - 1), device_id_type=MESH)

    @pl.when(high)
    def _():
        pl.semaphore_signal(barrier, inc=1, device_id=(me, my + 1), device_id_type=MESH)

    def greet(semaphore):
        def one(i, carry):
            pl.semaphore_signal(semaphore, inc=1, device_id=(lax.rem(me + i, nx), my), device_id_type=MESH)
            return carry

        lax.fori_loop(1, nx, one, 0)

    @pl.when(before)
    def _():
        greet(barrier)

    loads = [pltpu.make_async_copy(a, b, load_sem.at[i]) for i, (a, b) in enumerate(
        ((start, v_start), (lower, v_lower), (source, v_source), (diag, v_diag), (side, v_side), (upper, v_upper)))]
    for load in loads:
        load.start()

    def widen(x, top):
        lanes = lane_of(x.shape)
        turned = swap_halves(x)
        spread[pl.ds(top, 8 * nz // 16, stride=2), :] = jnp.where(lanes < 64, x, turned)
        spread[pl.ds(top + 1, 8 * nz // 16, stride=2), :] = jnp.where(lanes < 64, turned, x)
        return spread[top:top + nz, :]

    def narrow(x):
        spread[0:nz, :] = x
        even = spread[pl.ds(0, nz // 2, stride=2), :]
        odd = spread[pl.ds(1, nz // 2, stride=2), :]
        return jnp.where(lane_of(even.shape) < 64, even, odd)

    def shifted(x):
        pad[8:8 + nz, :] = x
        return pad[7:7 + nz, :], pad[9:9 + nz, :]

    pad[...] = jnp.zeros_like(pad)

    pick = jnp.where(lax.div(lax.rem(row_of((256, 128)), 128), 64) == lax.rem(lane_of((256, 128)), 2), 1.0, 0.0).astype(BF16)

    def apply(terms):
        out = jnp.zeros((nz, 128), F32)
        lanes = lax.div(lax.rem(lane_of((nz, 128)), 64), 2)
        for base in range(0, 32, CHUNK):
            pieces = []
            for c in range(base, base + CHUNK):
                total = None
                for block, vector in terms:
                    term = block[:, c * 128:(c + 1) * 128].astype(F32) * vector
                    total = term if total is None else total + term
                pieces.append(total)
            flat = jnp.concatenate(pieces, axis=0)
            high_part = flat.astype(BF16)
            low_part = (flat - high_part.astype(F32)).astype(BF16)
            sums = jnp.dot(jnp.concatenate([high_part, low_part], axis=1), pick, preferred_element_type=F32)
            for i in range(CHUNK):
                out = jnp.where(lanes == base + i, sums[i * nz:(i + 1) * nz, :], out)
        return out

    def square(z, slot):
        return cells[pl.ds(slot * 32 * nz + z, 32, stride=nz), :]

    def lay_out(block, slot, by=None):
        for c in range(32):
            piece = block[:, c * 128:(c + 1) * 128]
            piece = piece.astype(F32) if by is None else jnp.dot(piece, by, preferred_element_type=F32)
            cells[slot * 32 * nz + c * nz:slot * 32 * nz + (c + 1) * nz, :] = piece

    source_lane = row_of((128, 128))
    target = lax.div(source_lane, 64) * 64 + lax.rem(source_lane, 2) * 32 + lax.div(lax.rem(source_lane, 64), 2)
    sort = jnp.where(target == lane_of((128, 128)), 1.0, 0.0).astype(BF16)

    def compose(later, earlier, out):
        lay_out(later, 0, sort)
        lay_out(earlier, 1)
        lanes = lane_of((32, 128))
        for z in range(nz):
            b = square(z, 1)
            turned = swap_halves(b)
            right = jnp.concatenate([
                jnp.where(lanes < 64, b, 0.0), jnp.where(lanes < 64, turned, 0.0),
                jnp.where(lanes < 64, 0.0, turned), jnp.where(lanes < 64, 0.0, b)], axis=0).astype(BF16)
            out[z] = jnp.dot(square(z, 0).astype(BF16), right, preferred_element_type=F32)

    def compose_both(later, earlier, out, flip):
        @pl.when(jnp.logical_not(flip))
        def _():
            compose(later, earlier, out)

        @pl.when(flip)
        def _():
            compose_turned(later, earlier, out)

    order = jnp.where(lax.div(lane_of((64, 64)), 2) + 32 * lax.rem(lane_of((64, 64)), 2) == row_of((64, 64)), 1.0, 0.0).astype(BF16)

    unorder = jnp.where(lax.div(row_of((64, 64)), 2) + 32 * lax.rem(row_of((64, 64)), 2) == lane_of((64, 64)), 1.0, 0.0).astype(BF16)

    def compose_turned(later, earlier, out):
        lay_out(later, 0, sort)
        lay_out(earlier, 1)
        nt = (((1,), (1,)), ((), ()))
        for z in range(nz):
            a, b = square(z, 0), square(z, 1)
            a_stack = jnp.concatenate([a[:, :64], swap_halves(a)[:, :64]], axis=0).astype(BF16)
            b_stack = jnp.concatenate([b[:, :64], swap_halves(b)[:, :64]], axis=0).astype(BF16)
            b_turned = lax.dot_general(order, b_stack, nt, preferred_element_type=F32).astype(BF16)
            a_rows = jnp.dot(unorder, a_stack, preferred_element_type=F32).astype(BF16)
            turned = lax.dot_general(b_turned, a_rows, nt, preferred_element_type=F32)
            out[z] = jnp.concatenate([turned[:32], turned[32:]], axis=1)

    @pl.when(before)
    def _():
        loads[1].wait()
        compose_both(v_lower.at[1], v_lower.at[0], m_f, core == 1)

    pl.semaphore_wait(barrier, nx - 2 + low.astype(jnp.int32) + high.astype(jnp.int32) + (me == 0).astype(jnp.int32))

    @pl.when(me == 0)
    def _():
        greet(hello)
        loads[1].wait()

    loads[0].wait()

    def copy(src, dst, send, recv, where):
        return pltpu.make_async_remote_copy(src_ref=src, dst_ref=dst, send_sem=send, recv_sem=recv,
                                            device_id=where, device_id_type=MESH)

    @pl.when(low)
    def _():
        copy(v_start, halo_up, halo_send.at[0], halo_recv.at[0], (me, my - 1)).start()

    @pl.when(high)
    def _():
        copy(v_start, halo_dn, halo_send.at[1], halo_recv.at[1], (me, my + 1)).start()

    @pl.when(me >= 2)
    def _():
        copy(v_start.at[0], ahead, halo_send.at[2], halo_recv.at[2], (me - 1, my)).start()

    offsets = sorted(
        (-min(rx, edge - rx) - min(ry, edge - ry), ry, rx) for ry in range(edge) for rx in range(edge))
    half = edge // 2
    near = [(hops, ry, rx) for hops, ry, rx in offsets if -hops < half or (-hops == half and 1 <= rx <= half)]

    def beyond(ry, rx):
        return lax.rem(lax.div(chip, edge) + ry, edge) * edge + lax.rem(lax.rem(chip, edge) + rx, edge)

    def send_to(hops, which, src, dst, send, recv, to):
        if hops:
            copy(src, dst, send, recv, (to, my)).start()
        else:
            @pl.when(core != which)
            def _():
                copy(src, dst, send, recv, (to, my)).start()

            @pl.when(core == which)
            def _():
                pltpu.make_async_copy(src, dst, recv).start()

    def to_owners(rows, index, send, recv):
        inbox = (m_in if rows.shape[1] == 32 else b_in).at[index, slots[index]]
        for hops, ry, rx in offsets:
            there = beyond(ry, rx)
            if index == 0:
                send_to(hops, 1, rows.at[there], inbox, send.at[0], recv.at[0], 2 * there + 1)
            else:
                send_to(hops, 0, rows.at[there], inbox, send.at[1], recv.at[1], 2 * there)
                send_to(hops, 1, rows.at[opposite(there)], inbox, send.at[1], recv.at[1], 2 * there + 1)

    def from_owner(boxes, index):
        box = boxes.at[chip if index == 0 else line]
        for hops, ry, rx in (offsets if index == 0 else near):
            for which in range(2):
                to = 2 * beyond(ry, rx) + which
                step = to if index == 0 else nx - 1 - to
                send_to(hops, which, state.at[index, step], box, e_send.at[index], e_recv.at[index], to)

    def landed(ref, sem):
        pltpu.make_async_copy(ref, ref, sem).wait()

    slots = (me, nx - 1 - me)

    @pl.when(before)
    def _():
        to_owners(m_f, 0, m_send, m_recv)

    @pl.when(me == 1)
    def _():
        pl.semaphore_wait(hello, 1)
        copy(v_start.at[0], ahead, halo_send.at[2], halo_recv.at[2], (me - 1, my)).start()

    loads[2].wait()
    loads[3].wait()
    loads[4].wait()
    loads[5].wait()
    mine = [widen(v_start[p], 0) for p in range(2)]
    rhs = [apply([(v_diag.at[p], widen(v_source[p], 0))]) for p in range(2)]

    @pl.when(jnp.logical_not(low))
    def _():
        halo_dn[...] = jnp.zeros_like(halo_dn)

    @pl.when(jnp.logical_not(high))
    def _():
        halo_up[...] = jnp.zeros_like(halo_up)

    @pl.when(last)
    def _():
        ahead[...] = jnp.zeros_like(ahead)

    @pl.when(high)
    def _():
        landed(halo_up, halo_recv.at[0])

    @pl.when(low)
    def _():
        landed(halo_dn, halo_recv.at[1])

    @pl.when(jnp.logical_not(last))
    def _():
        landed(ahead, halo_recv.at[2])

    next_plane = [mine[1], widen(ahead[...], 0)]
    fixed, drive = [], []
    for p in range(2):
        below, above = shifted(mine[p])
        fixed.append(apply([(v_side.at[0, p], widen(halo_dn[p], 0)), (v_side.at[1, p], widen(halo_up[p], 0)),
                            (v_side.at[2, p], below), (v_side.at[3, p], above), (v_upper.at[p], next_plane[p])]))
        drive.append(rhs[p] - fixed[p])

    def put(rows, value):
        for z in range(nz):
            rows[z] = value[z:z + 1, :]

    def take(boxes, which):
        return jnp.concatenate([boxes[z, which] for z in range(nz)], axis=0)

    put(b_f, drive[1] - apply([(v_lower.at[1], drive[0])]))
    to_owners(b_f, 0, b_send, b_recv)

    @pl.when(me >= 2)
    def _():
        pl.semaphore_wait(hello, 1)

    compose_both(v_upper.at[0], v_upper.at[1], m_b, core == 0)
    to_owners(m_b, 1, m_send, m_recv)

    def chain(boxes, index):
        if index == 0:
            landed(m_in.at[0, pl.ds(0, nx - 1)], m_recv.at[0])
            m_in[0, 0] = jnp.zeros((32, 128), F32)
        else:
            landed(m_in.at[1], m_recv.at[1])
        lanes = lane_of((32, 128))
        rows = row_of((32, 128))
        left = lanes < 64
        even_place = lax.rem(lanes, 64) == 2 * rows
        odd_place = lax.rem(lanes, 64) == 2 * rows + 1
        left_row = lane_of((1, 128)) < 64

        def double(j, carry):
            a = m_in[index, 2 * j]
            turned = swap_halves(a)
            m_in[index, 2 * j] = jnp.where(left, a, turned)
            m_odd[j] = jnp.where(left, turned, a)
            return carry

        lax.fori_loop(0, nx // 2, double, 0, unroll=4)
        landed(b_in.at[index], b_recv.at[index])

        def pair(j, x):
            b = jnp.broadcast_to(b_in[index, 2 * j], (32, 128))
            x_rows = jnp.broadcast_to(x, (32, 128))
            even = jnp.sum(m_in[index, 2 * j] * x_rows
                           + jnp.where(jnp.logical_and(left, even_place), b, 0.0), axis=1, keepdims=True)
            odd = jnp.sum(m_odd[j] * x_rows
                          + jnp.where(jnp.logical_and(left, odd_place), b, 0.0), axis=1, keepdims=True)
            even, odd = jnp.broadcast_to(even, (32, 128)), jnp.broadcast_to(odd, (32, 128))
            y = (jnp.sum(m_in[index, 2 * j + 1] * jnp.where(left, even, odd), axis=0, keepdims=True)
                 + jnp.where(left_row, b_in[index, 2 * j + 1], 0.0))
            middle = jnp.sum(jnp.where(even_place, even, jnp.where(odd_place, odd, 0.0)), axis=0, keepdims=True)
            state[index, 2 * j, 0] = x + swap_halves(x)
            state[index, 2 * j, 1] = middle
            state[index, 2 * j + 1, 0] = middle
            state[index, 2 * j + 1, 1] = y + swap_halves(y)
            return y

        lax.fori_loop(0, nx // 2, pair, jnp.zeros((1, 128), F32), unroll=True)
        from_owner(boxes, index)

    @pl.when(core == 1)
    def _():
        chain(e_f, 0)

    landed(e_f, e_recv.at[0])
    f = [drive[0] - apply([(v_lower.at[0], take(e_f, 0))]), take(e_f, 1)]
    for p in range(2):
        f_mine[p] = f[p]

    @pl.when(low)
    def _():
        copy(f_mine, f_up, f_send.at[0], f_recv.at[0], (me, my - 1)).start()

    @pl.when(high)
    def _():
        copy(f_mine, f_dn, f_send.at[1], f_recv.at[1], (me, my + 1)).start()

    @pl.when(jnp.logical_not(low))
    def _():
        f_dn[...] = jnp.zeros_like(f_dn)

    @pl.when(jnp.logical_not(high))
    def _():
        f_up[...] = jnp.zeros_like(f_up)

    partial = []
    for p in range(2):
        forward_out[p] = narrow(f[p])
        below, above = shifted(f[p])
        partial.append(fixed[p] + f[p] - apply([(v_side.at[2, p], below), (v_side.at[3, p], above)]))

    @pl.when(high)
    def _():
        landed(f_up, f_recv.at[0])

    @pl.when(low)
    def _():
        landed(f_dn, f_recv.at[1])

    g = [partial[p] - apply([(v_side.at[0, p], f_dn[p]), (v_side.at[1, p], f_up[p])]) for p in range(2)]
    put(b_b, g[0] - apply([(v_upper.at[0], g[1])]))
    to_owners(b_b, 1, b_send, b_recv)
    chain(e_b, 1)

    landed(e_b, e_recv.at[1])
    result_out[0] = narrow(take(e_b, 1))
    result_out[1] = narrow(g[1] - apply([(v_upper.at[1], take(e_b, 0))]))

    @pl.when(low)
    def _():
        landed(v_start, halo_send.at[0])
        landed(f_mine, f_send.at[0])

    @pl.when(high)
    def _():
        landed(v_start, halo_send.at[1])
        landed(f_mine, f_send.at[1])

    @pl.when(before)
    def _():
        landed(ahead, halo_send.at[2])

    @pl.when(core == 1)
    def _():
        landed(m_f.at[pl.ds(0, nz - 1)], m_send.at[0])
        landed(b_f.at[pl.ds(0, nz - 1)], b_send.at[0])
        landed(state.at[0, pl.ds(0, nx - 1)], e_send.at[0])

    @pl.when(core == 0)
    def _():
        landed(b_f, b_send.at[0])

    @pl.when(jnp.logical_and(core == 0, before))
    def _():
        landed(m_f, m_send.at[0])

    landed(m_in.at[1, pl.ds(0, nx - 1)], m_send.at[1])
    landed(b_in.at[1, pl.ds(0, nx - 1)], b_send.at[1])
    landed(state.at[1, pl.ds(0, nz - 1)], e_send.at[1])


def hand_out(forward_in, result_in, forward_out, result_out):
    forward_out[...] = forward_in[...]
    result_out[...] = result_in[...]


def solution(mesh):
    nx, ny = mesh.shape["gx"], mesh.shape["gy"]

    def local(start, source, diag, lower, upper, side):
        nz = lower.shape[2]
        half = nz // 2
        width = lower.shape[3]
        any_space = pl.BlockSpec(memory_space=pl.ANY)
        vmem = pl.BlockSpec(memory_space=pltpu.VMEM)
        out = jax.ShapeDtypeStruct((2, half, 128), F32)
        dma = pltpu.SemaphoreType.DMA
        forward, result = pl.pallas_call(
            functools.partial(kernel, nx, ny, nz),
            out_shape=(pltpu.VMEM((2, half, 128), F32), pltpu.VMEM((2, half, 128), F32)),
            in_specs=[any_space] * 6,
            out_specs=(vmem, vmem),
            scratch_shapes=[
                pltpu.VMEM((2, half, 128), F32), pltpu.VMEM((2, half, 128), F32),
                pltpu.VMEM((2, nz, width), BF16), pltpu.VMEM((2, nz, width), BF16), pltpu.VMEM((2, nz, width), BF16),
                pltpu.VMEM((4, 2, nz, width), BF16),
                pltpu.VMEM((2, half, 128), F32), pltpu.VMEM((2, half, 128), F32), pltpu.VMEM((half, 128), F32),
                pltpu.VMEM((nz + 16, 128), F32), pltpu.VMEM((nz, 128), F32), pltpu.VMEM((2 * 32 * nz, 128), F32),
                pltpu.VMEM((nz, 32, 128), F32), pltpu.VMEM((nz, 32, 128), F32), pltpu.VMEM((2, nx, 32, 128), F32),
                pltpu.VMEM((nz, 1, 128), F32), pltpu.VMEM((nz, 1, 128), F32), pltpu.VMEM((2, nx, 1, 128), F32),
                pltpu.VMEM((2, nx, 2, 1, 128), F32),
                pltpu.VMEM((nz, 2, 1, 128), F32), pltpu.VMEM((nz, 2, 1, 128), F32), pltpu.VMEM((nx // 2, 32, 128), F32),
                pltpu.VMEM((2, nz, 128), F32), pltpu.VMEM((2, nz, 128), F32), pltpu.VMEM((2, nz, 128), F32),
                dma((6,)), dma((3,)), dma((3,)), dma((2,)), dma((2,)), dma((2,)), dma((2,)), dma((2,)), dma((2,)),
                dma((2,)), dma((2,)), pltpu.SemaphoreType.REGULAR,
            ],
            compiler_params=pltpu.CompilerParams(collective_id=0, has_side_effects=True),
        )(start.reshape(2, half, 128), source.reshape(2, half, 128), diag.reshape(2, nz, width),
          lower.reshape(2, nz, width), upper.reshape(2, nz, width), side.reshape(4, 2, nz, width))
        forward = pltpu.with_memory_space_constraint(forward, pltpu.VMEM)
        result = pltpu.with_memory_space_constraint(result, pltpu.VMEM)
        forward, result = pl.pallas_call(
            hand_out, out_shape=(out, out), in_specs=[vmem, vmem], out_specs=(vmem, vmem))(forward, result)
        return forward.reshape(start.shape), result.reshape(start.shape)

    return jax.shard_map(
        local,
        mesh=mesh,
        in_specs=(P("gx", "gy", None), P("gx", "gy", None), P("gx", "gy", None, None), P("gx", "gy", None, None),
                  P("gx", "gy", None, None), P(None, "gx", "gy", None, None)),
        out_specs=(P("gx", "gy", None), P("gx", "gy", None)),
        check_vma=False,
    )
```

```python
import functools

import jax
import jax.numpy as jnp
from jax import lax
from jax.experimental import pallas as pl
from jax.experimental.pallas import tpu as pltpu
from jax.sharding import PartitionSpec as P

MESH = pl.DeviceIdType.MESH
F32 = jnp.float32
BF16 = jnp.bfloat16
CHUNK = 8


def lane_of(shape):
    return lax.broadcasted_iota(jnp.int32, shape, len(shape) - 1)


def row_of(shape):
    return lax.broadcasted_iota(jnp.int32, shape, len(shape) - 2)


def swap_halves(x):
    return pltpu.roll(x, 64, 1)


def kernel(nx, ny, nz, *refs):
    (start, source, diag, lower, upper, side, forward_out, result_out,
     v_start, v_source, v_diag, v_lower, v_upper, v_side,
     halo_dn, halo_up, ahead, pad, spread, cells, m_f, m_b, m_in, b_f, b_b, b_in, state, e_f, e_b, m_odd, k_f, k_b,
     f_mine, f_dn, f_up,
     load_sem, halo_send, halo_recv, m_send, m_recv, b_send, b_recv, e_send, e_recv, f_send, f_recv,
     hello) = refs
    me, my = lax.axis_index("gx"), lax.axis_index("gy")
    core, chip = lax.rem(me, 2), lax.div(me, 2)
    low, high, before = my > 0, my < ny - 1, me > 0
    edge = 4 if nz == 16 else 2

    def opposite(place):
        half = edge // 2
        return lax.rem(lax.div(place, edge) + half, edge) * edge + lax.rem(lax.rem(place, edge) + half, edge)

    def line_at(place):
        y, x = lax.div(place, edge), lax.rem(place, edge)
        return y * edge + x + lax.rem(y, 2) * (edge - 1 - 2 * x)

    lines = (line_at(chip), line_at(opposite(chip)))
    last = me == nx - 1

    barrier = pltpu.get_barrier_semaphore()

    @pl.when(low)
    def _():
        pl.semaphore_signal(barrier, inc=1, device_id=(me, my - 1), device_id_type=MESH)

    @pl.when(high)
    def _():
        pl.semaphore_signal(barrier, inc=1, device_id=(me, my + 1), device_id_type=MESH)

    def greet(semaphore):
        def one(i, carry):
            pl.semaphore_signal(semaphore, inc=1, device_id=(lax.rem(me + i, nx), my), device_id_type=MESH)
            return carry

        lax.fori_loop(1, nx, one, 0)

    @pl.when(before)
    def _():
        greet(barrier)

    loads = [pltpu.make_async_copy(a, b, load_sem.at[i]) for i, (a, b) in enumerate(
        ((start, v_start), (lower, v_lower), (source, v_source), (diag, v_diag), (side, v_side), (upper, v_upper)))]
    for load in loads:
        load.start()

    def widen(x, top):
        lanes = lane_of(x.shape)
        turned = swap_halves(x)
        spread[pl.ds(top, 8 * nz // 16, stride=2), :] = jnp.where(lanes < 64, x, turned)
        spread[pl.ds(top + 1, 8 * nz // 16, stride=2), :] = jnp.where(lanes < 64, turned, x)
        return spread[top:top + nz, :]

    def narrow(x):
        spread[0:nz, :] = x
        even = spread[pl.ds(0, nz // 2, stride=2), :]
        odd = spread[pl.ds(1, nz // 2, stride=2), :]
        return jnp.where(lane_of(even.shape) < 64, even, odd)

    def shifted(x):
        pad[8:8 + nz, :] = x
        return pad[7:7 + nz, :], pad[9:9 + nz, :]

    pad[...] = jnp.zeros_like(pad)

    pick = jnp.where(lax.div(lax.rem(row_of((256, 128)), 128), 64) == lax.rem(lane_of((256, 128)), 2), 1.0, 0.0).astype(BF16)

    def apply(terms):
        out = jnp.zeros((nz, 128), F32)
        lanes = lax.div(lax.rem(lane_of((nz, 128)), 64), 2)
        for base in range(0, 32, CHUNK):
            pieces = []
            for c in range(base, base + CHUNK):
                total = None
                for block, vector in terms:
                    part = block[c * nz:(c + 1) * nz, :] if block.shape[-1] == 128 else block[:, c * 128:(c + 1) * 128]
                    term = part.astype(F32) * vector
                    total = term if total is None else total + term
                pieces.append(total)
            flat = jnp.concatenate(pieces, axis=0)
            high_part = flat.astype(BF16)
            low_part = (flat - high_part.astype(F32)).astype(BF16)
            sums = jnp.dot(jnp.concatenate([high_part, low_part], axis=1), pick, preferred_element_type=F32)
            for i in range(CHUNK):
                out = jnp.where(lanes == base + i, sums[i * nz:(i + 1) * nz, :], out)
        return out

    def square(z, slot):
        return cells[pl.ds(slot * 32 * nz + z, 32, stride=nz), :]

    def lay_out(block, slot, by=None):
        for c in range(32):
            piece = block[:, c * 128:(c + 1) * 128]
            piece = piece.astype(F32) if by is None else jnp.dot(piece, by, preferred_element_type=F32)
            cells[slot * 32 * nz + c * nz:slot * 32 * nz + (c + 1) * nz, :] = piece

    source_lane = row_of((128, 128))
    target = lax.div(source_lane, 64) * 64 + lax.rem(source_lane, 2) * 32 + lax.div(lax.rem(source_lane, 64), 2)
    sort = jnp.where(target == lane_of((128, 128)), 1.0, 0.0).astype(BF16)

    def compose_rows(later, earlier, out):
        compose(later, earlier, out, True)

    def compose(later, earlier, out, by_row=False):
        lay_out(later, 0, sort)
        lay_out(earlier, 1)
        lanes = lane_of((32, 128))
        for z in range(nz):
            b = square(z, 1)
            turned = swap_halves(b)
            right = jnp.concatenate([
                jnp.where(lanes < 64, b, 0.0), jnp.where(lanes < 64, turned, 0.0),
                jnp.where(lanes < 64, 0.0, turned), jnp.where(lanes < 64, 0.0, b)], axis=0).astype(BF16)
            product = jnp.dot(square(z, 0).astype(BF16), right, preferred_element_type=F32)
            if by_row:
                out[pl.ds(z, 32, stride=nz), :] = product
            else:
                out[z] = product

    def compose_both(later, earlier, out, flip):
        @pl.when(jnp.logical_not(flip))
        def _():
            compose(later, earlier, out)

        @pl.when(flip)
        def _():
            compose_turned(later, earlier, out)

    order = jnp.where(lax.div(lane_of((64, 64)), 2) + 32 * lax.rem(lane_of((64, 64)), 2) == row_of((64, 64)), 1.0, 0.0).astype(BF16)

    unorder = jnp.where(lax.div(row_of((64, 64)), 2) + 32 * lax.rem(row_of((64, 64)), 2) == lane_of((64, 64)), 1.0, 0.0).astype(BF16)

    def compose_turned(later, earlier, out):
        lay_out(later, 0, sort)
        lay_out(earlier, 1)
        nt = (((1,), (1,)), ((), ()))
        for z in range(nz):
            a, b = square(z, 0), square(z, 1)
            a_stack = jnp.concatenate([a[:, :64], swap_halves(a)[:, :64]], axis=0).astype(BF16)
            b_stack = jnp.concatenate([b[:, :64], swap_halves(b)[:, :64]], axis=0).astype(BF16)
            b_turned = lax.dot_general(order, b_stack, nt, preferred_element_type=F32).astype(BF16)
            a_rows = jnp.dot(unorder, a_stack, preferred_element_type=F32).astype(BF16)
            turned = lax.dot_general(b_turned, a_rows, nt, preferred_element_type=F32)
            out[z] = jnp.concatenate([turned[:32], turned[32:]], axis=1)

    @pl.when(before)
    def _():
        loads[1].wait()
        compose_both(v_lower.at[1], v_lower.at[0], m_f, core == 1)

    pl.semaphore_wait(barrier, nx - 2 + low.astype(jnp.int32) + high.astype(jnp.int32) + (me == 0).astype(jnp.int32))

    @pl.when(me == 0)
    def _():
        greet(hello)
        loads[1].wait()

    loads[0].wait()

    def copy(src, dst, send, recv, where):
        return pltpu.make_async_remote_copy(src_ref=src, dst_ref=dst, send_sem=send, recv_sem=recv,
                                            device_id=where, device_id_type=MESH)

    @pl.when(low)
    def _():
        copy(v_start, halo_up, halo_send.at[0], halo_recv.at[0], (me, my - 1)).start()

    @pl.when(high)
    def _():
        copy(v_start, halo_dn, halo_send.at[1], halo_recv.at[1], (me, my + 1)).start()

    @pl.when(me >= 2)
    def _():
        copy(v_start.at[0], ahead, halo_send.at[2], halo_recv.at[2], (me - 1, my)).start()

    offsets = sorted(
        (-min(rx, edge - rx) - min(ry, edge - ry), ry, rx) for ry in range(edge) for rx in range(edge))

    def beyond(ry, rx):
        return lax.rem(lax.div(chip, edge) + ry, edge) * edge + lax.rem(lax.rem(chip, edge) + rx, edge)

    def send_to(hops, which, src, dst, send, recv, to):
        if hops:
            copy(src, dst, send, recv, (to, my)).start()
        else:
            @pl.when(core != which)
            def _():
                copy(src, dst, send, recv, (to, my)).start()

            @pl.when(core == which)
            def _():
                pltpu.make_async_copy(src, dst, recv).start()

    def to_owners(rows, index, send, recv):
        inbox = (m_in if rows.shape[1] == 32 else b_in).at[slots[index]]
        for hops, ry, rx in offsets:
            there = beyond(ry, rx)
            z = line_at(there if index == 0 else opposite(there))
            send_to(hops, 1 - index, rows.at[z], inbox, send.at[index], recv.at[index], 2 * there + 1 - index)

    def from_owner(boxes, index):
        for hops, ry, rx in offsets:
            for which in range(2):
                to = 2 * beyond(ry, rx) + which
                step = to if index == 0 else nx - 1 - to
                send_to(hops, which, state.at[step], boxes.at[lines[index]], e_send, e_recv.at[index], to)

    def landed(ref, sem):
        pltpu.make_async_copy(ref, ref, sem).wait()

    slots = (me, nx - 1 - me)

    @pl.when(before)
    def _():
        to_owners(m_f, 0, m_send, m_recv)

    @pl.when(me == 1)
    def _():
        pl.semaphore_wait(hello, 1)
        copy(v_start.at[0], ahead, halo_send.at[2], halo_recv.at[2], (me - 1, my)).start()

    loads[2].wait()
    loads[3].wait()
    loads[4].wait()
    loads[5].wait()
    mine = [widen(v_start[p], 0) for p in range(2)]
    rhs = [apply([(v_diag.at[p], widen(v_source[p], 0))]) for p in range(2)]
    for q in range(2):
        compose_rows(v_lower.at[1], v_side.at[q, 0], k_f.at[q])
    fixed = []
    for p in range(2):
        below, above = shifted(mine[p])
        fixed.append(apply([(v_side.at[2, p], below), (v_side.at[3, p], above)]
                           + ([(v_upper.at[0], mine[1])] if p == 0 else [])))
    b_near = rhs[1] - fixed[1] - apply([(v_lower.at[1], rhs[0] - fixed[0])])

    @pl.when(jnp.logical_not(low))
    def _():
        halo_dn[...] = jnp.zeros_like(halo_dn)

    @pl.when(jnp.logical_not(high))
    def _():
        halo_up[...] = jnp.zeros_like(halo_up)

    @pl.when(last)
    def _():
        ahead[...] = jnp.zeros_like(ahead)

    @pl.when(high)
    def _():
        landed(halo_up, halo_recv.at[0])

    @pl.when(low)
    def _():
        landed(halo_dn, halo_recv.at[1])

    @pl.when(jnp.logical_not(last))
    def _():
        landed(ahead, halo_recv.at[2])

    def put(rows, value):
        for z in range(nz):
            rows[z] = value[z:z + 1, :]

    def take(boxes, which):
        return jnp.concatenate([boxes[z, which] for z in range(nz)], axis=0)

    dn = [widen(halo_dn[p], 0) for p in range(2)]
    up = [widen(halo_up[p], 0) for p in range(2)]
    next_plane = widen(ahead[...], 0)
    put(b_f, b_near - apply([(v_side.at[0, 1], dn[1]), (v_side.at[1, 1], up[1]), (v_upper.at[1], next_plane),
                             (k_f.at[0], -dn[0]), (k_f.at[1], -up[0])]))
    to_owners(b_f, 0, b_send, b_recv)
    for p in range(2):
        fixed[p] = fixed[p] + apply([(v_side.at[0, p], dn[p]), (v_side.at[1, p], up[p])]
                                    + ([(v_upper.at[1], next_plane)] if p == 1 else []))
    drive = [rhs[p] - fixed[p] for p in range(2)]

    @pl.when(me >= 2)
    def _():
        pl.semaphore_wait(hello, 1)

    compose_both(v_upper.at[0], v_upper.at[1], m_b, core == 0)
    to_owners(m_b, 1, m_send, m_recv)
    for q in range(2):
        compose_rows(v_upper.at[0], v_side.at[q, 1], k_b.at[q])

    def chain(boxes, index):
        if index == 0:
            landed(m_in.at[pl.ds(0, nx - 1)], m_recv.at[0])
            m_in[0] = jnp.zeros((32, 128), F32)
        else:
            landed(m_in, m_recv.at[1])
        lanes = lane_of((32, 128))
        rows = row_of((32, 128))
        left = lanes < 64
        even_place = lax.rem(lanes, 64) == 2 * rows
        odd_place = lax.rem(lanes, 64) == 2 * rows + 1
        left_row = lane_of((1, 128)) < 64

        def double(j, carry):
            a = m_in[2 * j]
            turned = swap_halves(a)
            m_in[2 * j] = jnp.where(left, a, turned)
            m_odd[j] = jnp.where(left, turned, a)
            return carry

        lax.fori_loop(0, nx // 2, double, 0, unroll=4)
        landed(b_in, b_recv.at[index])

        def pair(j, x):
            b = jnp.broadcast_to(b_in[2 * j], (32, 128))
            x_rows = jnp.broadcast_to(x, (32, 128))
            even = jnp.sum(m_in[2 * j] * x_rows
                           + jnp.where(jnp.logical_and(left, even_place), b, 0.0), axis=1, keepdims=True)
            odd = jnp.sum(m_odd[j] * x_rows
                          + jnp.where(jnp.logical_and(left, odd_place), b, 0.0), axis=1, keepdims=True)
            even, odd = jnp.broadcast_to(even, (32, 128)), jnp.broadcast_to(odd, (32, 128))
            y = (jnp.sum(m_in[2 * j + 1] * jnp.where(left, even, odd), axis=0, keepdims=True)
                 + jnp.where(left_row, b_in[2 * j + 1], 0.0))
            middle = jnp.sum(jnp.where(even_place, even, jnp.where(odd_place, odd, 0.0)), axis=0, keepdims=True)
            state[2 * j, 0] = x + swap_halves(x)
            state[2 * j, 1] = middle
            state[2 * j + 1, 0] = middle
            state[2 * j + 1, 1] = y + swap_halves(y)
            return y

        lax.fori_loop(0, nx // 2, pair, jnp.zeros((1, 128), F32), unroll=True)
        from_owner(boxes, index)

    @pl.when(core == 1)
    def _():
        chain(e_f, 0)

    landed(e_f, e_recv.at[0])
    f = [drive[0] - apply([(v_lower.at[0], take(e_f, 0))]), take(e_f, 1)]
    for p in range(2):
        f_mine[p] = f[p]

    @pl.when(low)
    def _():
        copy(f_mine, f_up, f_send.at[0], f_recv.at[0], (me, my - 1)).start()

    @pl.when(high)
    def _():
        copy(f_mine, f_dn, f_send.at[1], f_recv.at[1], (me, my + 1)).start()

    @pl.when(jnp.logical_not(low))
    def _():
        f_dn[...] = jnp.zeros_like(f_dn)

    @pl.when(jnp.logical_not(high))
    def _():
        f_up[...] = jnp.zeros_like(f_up)

    partial = []
    for p in range(2):
        forward_out[p] = narrow(f[p])
        below, above = shifted(f[p])
        partial.append(fixed[p] + f[p] - apply([(v_side.at[2, p], below), (v_side.at[3, p], above)]))

    b_near = partial[0] - apply([(v_upper.at[0], partial[1])])

    @pl.when(high)
    def _():
        landed(f_up, f_recv.at[0])

    @pl.when(low)
    def _():
        landed(f_dn, f_recv.at[1])

    dn, up = [f_dn[p] for p in range(2)], [f_up[p] for p in range(2)]
    put(b_b, b_near - apply([(v_side.at[0, 0], dn[0]), (v_side.at[1, 0], up[0]), (k_b.at[0], -dn[1]), (k_b.at[1], -up[1])]))
    to_owners(b_b, 1, b_send, b_recv)
    drive_1 = partial[1] - apply([(v_side.at[0, 1], dn[1]), (v_side.at[1, 1], up[1])])

    @pl.when(core == 0)
    def _():
        chain(e_b, 1)


    landed(e_b, e_recv.at[1])
    result_out[0] = narrow(take(e_b, 1))
    result_out[1] = narrow(drive_1 - apply([(v_upper.at[1], take(e_b, 0))]))

    @pl.when(low)
    def _():
        landed(v_start, halo_send.at[0])
        landed(f_mine, f_send.at[0])

    @pl.when(high)
    def _():
        landed(v_start, halo_send.at[1])
        landed(f_mine, f_send.at[1])

    @pl.when(before)
    def _():
        landed(ahead, halo_send.at[2])

    for index, rows, sem, sends in ((0, m_f, m_send, before), (0, b_f, b_send, True), (1, m_b, m_send, True), (1, b_b, b_send, True)):
        @pl.when(jnp.logical_and(core == 1 - index, sends))
        def _():
            landed(rows.at[pl.ds(0, nz - 1)], sem.at[index])

        @pl.when(jnp.logical_and(core == index, sends))
        def _():
            landed(rows, sem.at[index])

    landed(state.at[pl.ds(0, nx - 1)], e_send)


def hand_out(forward_in, result_in, forward_out, result_out):
    forward_out[...] = forward_in[...]
    result_out[...] = result_in[...]


def solution(mesh):
    nx, ny = mesh.shape["gx"], mesh.shape["gy"]

    def local(start, source, diag, lower, upper, side):
        nz = lower.shape[2]
        half = nz // 2
        width = lower.shape[3]
        any_space = pl.BlockSpec(memory_space=pl.ANY)
        vmem = pl.BlockSpec(memory_space=pltpu.VMEM)
        out = jax.ShapeDtypeStruct((2, half, 128), F32)
        dma = pltpu.SemaphoreType.DMA
        forward, result = pl.pallas_call(
            functools.partial(kernel, nx, ny, nz),
            out_shape=(pltpu.VMEM((2, half, 128), F32), pltpu.VMEM((2, half, 128), F32)),
            in_specs=[any_space] * 6,
            out_specs=(vmem, vmem),
            scratch_shapes=[
                pltpu.VMEM((2, half, 128), F32), pltpu.VMEM((2, half, 128), F32),
                pltpu.VMEM((2, nz, width), BF16), pltpu.VMEM((2, nz, width), BF16), pltpu.VMEM((2, nz, width), BF16),
                pltpu.VMEM((4, 2, nz, width), BF16),
                pltpu.VMEM((2, half, 128), F32), pltpu.VMEM((2, half, 128), F32), pltpu.VMEM((half, 128), F32),
                pltpu.VMEM((nz + 16, 128), F32), pltpu.VMEM((nz, 128), F32), pltpu.VMEM((2 * 32 * nz, 128), F32),
                pltpu.VMEM((nz, 32, 128), F32), pltpu.VMEM((nz, 32, 128), F32), pltpu.VMEM((nx, 32, 128), F32),
                pltpu.VMEM((nz, 1, 128), F32), pltpu.VMEM((nz, 1, 128), F32), pltpu.VMEM((nx, 1, 128), F32),
                pltpu.VMEM((nx, 2, 1, 128), F32),
                pltpu.VMEM((nz, 2, 1, 128), F32), pltpu.VMEM((nz, 2, 1, 128), F32), pltpu.VMEM((nx // 2, 32, 128), F32),
                pltpu.VMEM((2, 32 * nz, 128), F32), pltpu.VMEM((2, 32 * nz, 128), F32),
                pltpu.VMEM((2, nz, 128), F32), pltpu.VMEM((2, nz, 128), F32), pltpu.VMEM((2, nz, 128), F32),
                dma((6,)), dma((3,)), dma((3,)), dma((2,)), dma((2,)), dma((2,)), dma((2,)), dma, dma((2,)),
                dma((2,)), dma((2,)), pltpu.SemaphoreType.REGULAR,
            ],
            compiler_params=pltpu.CompilerParams(collective_id=0, has_side_effects=True),
        )(start.reshape(2, half, 128), source.reshape(2, half, 128), diag.reshape(2, nz, width),
          lower.reshape(2, nz, width), upper.reshape(2, nz, width), side.reshape(4, 2, nz, width))
        forward = pltpu.with_memory_space_constraint(forward, pltpu.VMEM)
        result = pltpu.with_memory_space_constraint(result, pltpu.VMEM)
        forward, result = pl.pallas_call(
            hand_out, out_shape=(out, out), in_specs=[vmem, vmem], out_specs=(vmem, vmem))(forward, result)
        return forward.reshape(start.shape), result.reshape(start.shape)

    return jax.shard_map(
        local,
        mesh=mesh,
        in_specs=(P("gx", "gy", None), P("gx", "gy", None), P("gx", "gy", None, None), P("gx", "gy", None, None),
                  P("gx", "gy", None, None), P(None, "gx", "gy", None, None)),
        out_specs=(P("gx", "gy", None), P("gx", "gy", None)),
        check_vma=False,
    )
```

```python
import functools

import jax
import jax.numpy as jnp
from jax import lax
from jax.experimental import pallas as pl
from jax.experimental.pallas import tpu as pltpu
from jax.sharding import PartitionSpec as P

MESH = pl.DeviceIdType.MESH
F32 = jnp.float32
BF16 = jnp.bfloat16
CHUNK = 8


def lane_of(shape):
    return lax.broadcasted_iota(jnp.int32, shape, len(shape) - 1)


def row_of(shape):
    return lax.broadcasted_iota(jnp.int32, shape, len(shape) - 2)


def swap_halves(x):
    return pltpu.roll(x, 64, 1)


def kernel(nx, ny, nz, *refs):
    (start, source, diag, lower, upper, side, forward_out, result_out,
     v_start, v_source, v_diag, v_lower, v_upper, v_side,
     halo_dn, halo_up, ahead, pad, spread, cells, m_f, m_b, m_in, b_f, b_b, b_in, state, e_f, e_b, m_odd, k_f, k_b,
     f_mine, f_dn, f_up,
     load_sem, halo_send, halo_recv, m_send, m_recv, b_send, b_recv, e_send, e_recv, f_send, f_recv,
     hello) = refs
    me, my = lax.axis_index("gx"), lax.axis_index("gy")
    core, chip = lax.rem(me, 2), lax.div(me, 2)
    low, high, before = my > 0, my < ny - 1, me > 0
    edge = 4 if nz == 16 else 2

    def opposite(place):
        half = edge // 2
        return lax.rem(lax.div(place, edge) + half, edge) * edge + lax.rem(lax.rem(place, edge) + half, edge)

    def line_at(place):
        y, x = lax.div(place, edge), lax.rem(place, edge)
        return y * edge + x + lax.rem(y, 2) * (edge - 1 - 2 * x)

    lines = (line_at(chip), line_at(opposite(chip)))
    last = me == nx - 1

    barrier = pltpu.get_barrier_semaphore()

    @pl.when(low)
    def _():
        pl.semaphore_signal(barrier, inc=1, device_id=(me, my - 1), device_id_type=MESH)

    @pl.when(high)
    def _():
        pl.semaphore_signal(barrier, inc=1, device_id=(me, my + 1), device_id_type=MESH)

    def greet(semaphore):
        def one(i, carry):
            pl.semaphore_signal(semaphore, inc=1, device_id=(lax.rem(me + i, nx), my), device_id_type=MESH)
            return carry

        lax.fori_loop(1, nx, one, 0)

    @pl.when(before)
    def _():
        greet(barrier)

    loads = [pltpu.make_async_copy(a, b, load_sem.at[i]) for i, (a, b) in enumerate(
        ((start, v_start), (lower, v_lower), (source, v_source), (diag, v_diag), (side, v_side), (upper, v_upper)))]
    for load in loads:
        load.start()

    def widen(x, top):
        lanes = lane_of(x.shape)
        turned = swap_halves(x)
        spread[pl.ds(top, 8 * nz // 16, stride=2), :] = jnp.where(lanes < 64, x, turned)
        spread[pl.ds(top + 1, 8 * nz // 16, stride=2), :] = jnp.where(lanes < 64, turned, x)
        return spread[top:top + nz, :]

    def narrow(x):
        spread[0:nz, :] = x
        even = spread[pl.ds(0, nz // 2, stride=2), :]
        odd = spread[pl.ds(1, nz // 2, stride=2), :]
        return jnp.where(lane_of(even.shape) < 64, even, odd)

    def shifted(x):
        pad[8:8 + nz, :] = x
        return pad[7:7 + nz, :], pad[9:9 + nz, :]

    pad[...] = jnp.zeros_like(pad)

    pick = jnp.where(lax.div(lax.rem(row_of((256, 128)), 128), 64) == lax.rem(lane_of((256, 128)), 2), 1.0, 0.0).astype(BF16)

    def apply(terms):
        out = jnp.zeros((nz, 128), F32)
        lanes = lax.div(lax.rem(lane_of((nz, 128)), 64), 2)
        for base in range(0, 32, CHUNK):
            pieces = []
            for c in range(base, base + CHUNK):
                total = None
                for block, vector in terms:
                    part = block[c * nz:(c + 1) * nz, :] if block.shape[-1] == 128 else block[:, c * 128:(c + 1) * 128]
                    term = part.astype(F32) * vector
                    total = term if total is None else total + term
                pieces.append(total)
            flat = jnp.concatenate(pieces, axis=0)
            high_part = flat.astype(BF16)
            low_part = (flat - high_part.astype(F32)).astype(BF16)
            sums = jnp.dot(jnp.concatenate([high_part, low_part], axis=1), pick, preferred_element_type=F32)
            for i in range(CHUNK):
                out = jnp.where(lanes == base + i, sums[i * nz:(i + 1) * nz, :], out)
        return out

    def square(z, slot):
        return cells[pl.ds(slot * 32 * nz + z, 32, stride=nz), :]

    def lay_out(block, slot, by=None):
        for c in range(32):
            piece = block[:, c * 128:(c + 1) * 128]
            piece = piece.astype(F32) if by is None else jnp.dot(piece, by, preferred_element_type=F32)
            cells[slot * 32 * nz + c * nz:slot * 32 * nz + (c + 1) * nz, :] = piece

    source_lane = row_of((128, 128))
    target = lax.div(source_lane, 64) * 64 + lax.rem(source_lane, 2) * 32 + lax.div(lax.rem(source_lane, 64), 2)
    sort = jnp.where(target == lane_of((128, 128)), 1.0, 0.0).astype(BF16)

    def compose_rows(later, earlier, out):
        compose(later, earlier, out, True)

    def compose(later, earlier, out, by_row=False):
        lay_out(later, 0, sort)
        lay_out(earlier, 1)
        lanes = lane_of((32, 128))
        for z in range(nz):
            b = square(z, 1)
            turned = swap_halves(b)
            right = jnp.concatenate([
                jnp.where(lanes < 64, b, 0.0), jnp.where(lanes < 64, turned, 0.0),
                jnp.where(lanes < 64, 0.0, turned), jnp.where(lanes < 64, 0.0, b)], axis=0).astype(BF16)
            product = jnp.dot(square(z, 0).astype(BF16), right, preferred_element_type=F32)
            if by_row:
                out[pl.ds(z, 32, stride=nz), :] = product
            else:
                out[z] = product

    def compose_both(later, earlier, out, flip):
        @pl.when(jnp.logical_not(flip))
        def _():
            compose(later, earlier, out)

        @pl.when(flip)
        def _():
            compose_turned(later, earlier, out)

    order = jnp.where(lax.div(lane_of((64, 64)), 2) + 32 * lax.rem(lane_of((64, 64)), 2) == row_of((64, 64)), 1.0, 0.0).astype(BF16)

    unorder = jnp.where(lax.div(row_of((64, 64)), 2) + 32 * lax.rem(row_of((64, 64)), 2) == lane_of((64, 64)), 1.0, 0.0).astype(BF16)

    def compose_turned(later, earlier, out):
        lay_out(later, 0, sort)
        lay_out(earlier, 1)
        nt = (((1,), (1,)), ((), ()))
        for z in range(nz):
            a, b = square(z, 0), square(z, 1)
            a_stack = jnp.concatenate([a[:, :64], swap_halves(a)[:, :64]], axis=0).astype(BF16)
            b_stack = jnp.concatenate([b[:, :64], swap_halves(b)[:, :64]], axis=0).astype(BF16)
            b_turned = lax.dot_general(order, b_stack, nt, preferred_element_type=F32).astype(BF16)
            a_rows = jnp.dot(unorder, a_stack, preferred_element_type=F32).astype(BF16)
            turned = lax.dot_general(b_turned, a_rows, nt, preferred_element_type=F32)
            out[z] = jnp.concatenate([turned[:32], turned[32:]], axis=1)

    @pl.when(before)
    def _():
        loads[1].wait()
        compose_both(v_lower.at[1], v_lower.at[0], m_f, core == 1)

    pl.semaphore_wait(barrier, nx - 2 + low.astype(jnp.int32) + high.astype(jnp.int32) + (me == 0).astype(jnp.int32))

    loads[0].wait()

    def copy(src, dst, send, recv, where):
        return pltpu.make_async_remote_copy(src_ref=src, dst_ref=dst, send_sem=send, recv_sem=recv,
                                            device_id=where, device_id_type=MESH)

    @pl.when(low)
    def _():
        copy(v_start, halo_up, halo_send.at[0], halo_recv.at[0], (me, my - 1)).start()

    @pl.when(high)
    def _():
        copy(v_start, halo_dn, halo_send.at[1], halo_recv.at[1], (me, my + 1)).start()

    @pl.when(me == 0)
    def _():
        greet(hello)
        loads[1].wait()

    @pl.when(me >= 2)
    def _():
        copy(v_start.at[0], ahead, halo_send.at[2], halo_recv.at[2], (me - 1, my)).start()

    offsets = sorted(
        (-min(rx, edge - rx) - min(ry, edge - ry), ry, rx) for ry in range(edge) for rx in range(edge))

    def beyond(ry, rx):
        return lax.rem(lax.div(chip, edge) + ry, edge) * edge + lax.rem(lax.rem(chip, edge) + rx, edge)

    def send_to(hops, which, src, dst, send, recv, to):
        if hops:
            copy(src, dst, send, recv, (to, my)).start()
        else:
            @pl.when(core != which)
            def _():
                copy(src, dst, send, recv, (to, my)).start()

            @pl.when(core == which)
            def _():
                pltpu.make_async_copy(src, dst, recv).start()

    def to_owners(rows, index, send, recv):
        inbox = (m_in if rows.shape[1] == 32 else b_in).at[slots[index]]
        for hops, ry, rx in offsets:
            there = beyond(ry, rx)
            z = line_at(there if index == 0 else opposite(there))
            send_to(hops, 1 - index, rows.at[z], inbox, send.at[index], recv.at[index], 2 * there + 1 - index)

    def from_owner(boxes, index):
        for hops, ry, rx in offsets:
            for which in range(2):
                to = 2 * beyond(ry, rx) + which
                step = to if index == 0 else nx - 1 - to
                send_to(hops, which, state.at[step], boxes.at[lines[index]], e_send, e_recv.at[index], to)

    def landed(ref, sem):
        pltpu.make_async_copy(ref, ref, sem).wait()

    slots = (me, nx - 1 - me)

    @pl.when(before)
    def _():
        to_owners(m_f, 0, m_send, m_recv)

    @pl.when(me == 1)
    def _():
        pl.semaphore_wait(hello, 1)
        copy(v_start.at[0], ahead, halo_send.at[2], halo_recv.at[2], (me - 1, my)).start()

    loads[2].wait()
    loads[3].wait()
    loads[4].wait()
    loads[5].wait()
    mine = [widen(v_start[p], 0) for p in range(2)]
    rhs = [apply([(v_diag.at[p], widen(v_source[p], 0))]) for p in range(2)]
    for q in range(2):
        compose_rows(v_lower.at[1], v_side.at[q, 0], k_f.at[q])
    fixed = []
    for p in range(2):
        below, above = shifted(mine[p])
        fixed.append(apply([(v_side.at[2, p], below), (v_side.at[3, p], above)]
                           + ([(v_upper.at[0], mine[1])] if p == 0 else [])))
    b_near = rhs[1] - fixed[1] - apply([(v_lower.at[1], rhs[0] - fixed[0])])

    @pl.when(jnp.logical_not(low))
    def _():
        halo_dn[...] = jnp.zeros_like(halo_dn)

    @pl.when(jnp.logical_not(high))
    def _():
        halo_up[...] = jnp.zeros_like(halo_up)

    @pl.when(last)
    def _():
        ahead[...] = jnp.zeros_like(ahead)

    @pl.when(high)
    def _():
        landed(halo_up, halo_recv.at[0])

    @pl.when(low)
    def _():
        landed(halo_dn, halo_recv.at[1])

    @pl.when(jnp.logical_not(last))
    def _():
        landed(ahead, halo_recv.at[2])

    def put(rows, value):
        for z in range(nz):
            rows[z] = value[z:z + 1, :]

    def take(boxes, which):
        return jnp.concatenate([boxes[z, which] for z in range(nz)], axis=0)

    dn = [widen(halo_dn[p], 0) for p in range(2)]
    up = [widen(halo_up[p], 0) for p in range(2)]
    next_plane = widen(ahead[...], 0)
    put(b_f, b_near - apply([(v_side.at[0, 1], dn[1]), (v_side.at[1, 1], up[1]), (v_upper.at[1], next_plane),
                             (k_f.at[0], -dn[0]), (k_f.at[1], -up[0])]))
    to_owners(b_f, 0, b_send, b_recv)
    for p in range(2):
        fixed[p] = fixed[p] + apply([(v_side.at[0, p], dn[p]), (v_side.at[1, p], up[p])]
                                    + ([(v_upper.at[1], next_plane)] if p == 1 else []))
    drive = [rhs[p] - fixed[p] for p in range(2)]

    @pl.when(me >= 2)
    def _():
        pl.semaphore_wait(hello, 1)

    compose_both(v_upper.at[0], v_upper.at[1], m_b, core == 0)
    to_owners(m_b, 1, m_send, m_recv)
    for q in range(2):
        compose_rows(v_upper.at[0], v_side.at[q, 1], k_b.at[q])

    def chain(boxes, index):
        if index == 0:
            landed(m_in.at[pl.ds(0, nx - 1)], m_recv.at[0])
            m_in[0] = jnp.zeros((32, 128), F32)
        else:
            landed(m_in, m_recv.at[1])
        lanes = lane_of((32, 128))
        rows = row_of((32, 128))
        left = lanes < 64
        even_place = lax.rem(lanes, 64) == 2 * rows
        odd_place = lax.rem(lanes, 64) == 2 * rows + 1
        left_row = lane_of((1, 128)) < 64

        def double(j, carry):
            a = m_in[2 * j]
            turned = swap_halves(a)
            m_in[2 * j] = jnp.where(left, a, turned)
            m_odd[j] = jnp.where(left, turned, a)
            return carry

        lax.fori_loop(0, nx // 2, double, 0, unroll=4)
        landed(b_in, b_recv.at[index])

        def pair(j, x):
            b = jnp.broadcast_to(b_in[2 * j], (32, 128))
            x_rows = jnp.broadcast_to(x, (32, 128))
            even = jnp.sum(m_in[2 * j] * x_rows
                           + jnp.where(jnp.logical_and(left, even_place), b, 0.0), axis=1, keepdims=True)
            odd = jnp.sum(m_odd[j] * x_rows
                          + jnp.where(jnp.logical_and(left, odd_place), b, 0.0), axis=1, keepdims=True)
            even, odd = jnp.broadcast_to(even, (32, 128)), jnp.broadcast_to(odd, (32, 128))
            y = (jnp.sum(m_in[2 * j + 1] * jnp.where(left, even, odd), axis=0, keepdims=True)
                 + jnp.where(left_row, b_in[2 * j + 1], 0.0))
            middle = jnp.sum(jnp.where(even_place, even, jnp.where(odd_place, odd, 0.0)), axis=0, keepdims=True)
            state[2 * j, 0] = x + swap_halves(x)
            state[2 * j, 1] = middle
            state[2 * j + 1, 0] = middle
            state[2 * j + 1, 1] = y + swap_halves(y)
            return y

        lax.fori_loop(0, nx // 2, pair, jnp.zeros((1, 128), F32), unroll=True)
        from_owner(boxes, index)

    @pl.when(core == 1)
    def _():
        chain(e_f, 0)

    landed(e_f, e_recv.at[0])
    f = [drive[0] - apply([(v_lower.at[0], take(e_f, 0))]), take(e_f, 1)]
    for p in range(2):
        f_mine[p] = f[p]

    @pl.when(low)
    def _():
        copy(f_mine, f_up, f_send.at[0], f_recv.at[0], (me, my - 1)).start()

    @pl.when(high)
    def _():
        copy(f_mine, f_dn, f_send.at[1], f_recv.at[1], (me, my + 1)).start()

    @pl.when(jnp.logical_not(low))
    def _():
        f_dn[...] = jnp.zeros_like(f_dn)

    @pl.when(jnp.logical_not(high))
    def _():
        f_up[...] = jnp.zeros_like(f_up)

    partial = []
    for p in range(2):
        forward_out[p] = narrow(f[p])
        below, above = shifted(f[p])
        partial.append(fixed[p] + f[p] - apply([(v_side.at[2, p], below), (v_side.at[3, p], above)]))

    b_near = partial[0] - apply([(v_upper.at[0], partial[1])])

    @pl.when(high)
    def _():
        landed(f_up, f_recv.at[0])

    @pl.when(low)
    def _():
        landed(f_dn, f_recv.at[1])

    dn, up = [f_dn[p] for p in range(2)], [f_up[p] for p in range(2)]
    put(b_b, b_near - apply([(v_side.at[0, 0], dn[0]), (v_side.at[1, 0], up[0]), (k_b.at[0], -dn[1]), (k_b.at[1], -up[1])]))
    to_owners(b_b, 1, b_send, b_recv)
    drive_1 = partial[1] - apply([(v_side.at[0, 1], dn[1]), (v_side.at[1, 1], up[1])])

    @pl.when(core == 0)
    def _():
        chain(e_b, 1)


    landed(e_b, e_recv.at[1])
    result_out[0] = narrow(take(e_b, 1))
    result_out[1] = narrow(drive_1 - apply([(v_upper.at[1], take(e_b, 0))]))

    @pl.when(low)
    def _():
        landed(v_start, halo_send.at[0])
        landed(f_mine, f_send.at[0])

    @pl.when(high)
    def _():
        landed(v_start, halo_send.at[1])
        landed(f_mine, f_send.at[1])

    @pl.when(before)
    def _():
        landed(ahead, halo_send.at[2])

    for index, rows, sem, sends in ((0, m_f, m_send, before), (0, b_f, b_send, True), (1, m_b, m_send, True), (1, b_b, b_send, True)):
        @pl.when(jnp.logical_and(core == 1 - index, sends))
        def _():
            landed(rows.at[pl.ds(0, nz - 1)], sem.at[index])

        @pl.when(jnp.logical_and(core == index, sends))
        def _():
            landed(rows, sem.at[index])

    landed(state.at[pl.ds(0, nx - 1)], e_send)


def hand_out(forward_in, result_in, forward_out, result_out, sem):
    copies = [pltpu.make_async_copy(forward_in, forward_out, sem.at[0]),
              pltpu.make_async_copy(result_in, result_out, sem.at[1])]
    for one in copies:
        one.start()
    for one in copies:
        one.wait()


def solution(mesh):
    nx, ny = mesh.shape["gx"], mesh.shape["gy"]

    def local(start, source, diag, lower, upper, side):
        nz = lower.shape[2]
        half = nz // 2
        width = lower.shape[3]
        any_space = pl.BlockSpec(memory_space=pl.ANY)
        vmem = pl.BlockSpec(memory_space=pltpu.VMEM)
        out = jax.ShapeDtypeStruct((2, half, 128), F32)
        dma = pltpu.SemaphoreType.DMA
        forward, result = pl.pallas_call(
            functools.partial(kernel, nx, ny, nz),
            out_shape=(pltpu.VMEM((2, half, 128), F32), pltpu.VMEM((2, half, 128), F32)),
            in_specs=[any_space] * 6,
            out_specs=(vmem, vmem),
            scratch_shapes=[
                pltpu.VMEM((2, half, 128), F32), pltpu.VMEM((2, half, 128), F32),
                pltpu.VMEM((2, nz, width), BF16), pltpu.VMEM((2, nz, width), BF16), pltpu.VMEM((2, nz, width), BF16),
                pltpu.VMEM((4, 2, nz, width), BF16),
                pltpu.VMEM((2, half, 128), F32), pltpu.VMEM((2, half, 128), F32), pltpu.VMEM((half, 128), F32),
                pltpu.VMEM((nz + 16, 128), F32), pltpu.VMEM((nz, 128), F32), pltpu.VMEM((2 * 32 * nz, 128), F32),
                pltpu.VMEM((nz, 32, 128), F32), pltpu.VMEM((nz, 32, 128), F32), pltpu.VMEM((nx, 32, 128), F32),
                pltpu.VMEM((nz, 1, 128), F32), pltpu.VMEM((nz, 1, 128), F32), pltpu.VMEM((nx, 1, 128), F32),
                pltpu.VMEM((nx, 2, 1, 128), F32),
                pltpu.VMEM((nz, 2, 1, 128), F32), pltpu.VMEM((nz, 2, 1, 128), F32), pltpu.VMEM((nx // 2, 32, 128), F32),
                pltpu.VMEM((2, 32 * nz, 128), F32), pltpu.VMEM((2, 32 * nz, 128), F32),
                pltpu.VMEM((2, nz, 128), F32), pltpu.VMEM((2, nz, 128), F32), pltpu.VMEM((2, nz, 128), F32),
                dma((6,)), dma((3,)), dma((3,)), dma((2,)), dma((2,)), dma((2,)), dma((2,)), dma, dma((2,)),
                dma((2,)), dma((2,)), pltpu.SemaphoreType.REGULAR,
            ],
            compiler_params=pltpu.CompilerParams(collective_id=0, has_side_effects=True),
        )(start.reshape(2, half, 128), source.reshape(2, half, 128), diag.reshape(2, nz, width),
          lower.reshape(2, nz, width), upper.reshape(2, nz, width), side.reshape(4, 2, nz, width))
        forward = pltpu.with_memory_space_constraint(forward, pltpu.VMEM)
        result = pltpu.with_memory_space_constraint(result, pltpu.VMEM)
        forward, result = pl.pallas_call(
            hand_out, out_shape=(out, out), in_specs=[vmem, vmem], out_specs=(any_space, any_space),
            scratch_shapes=[dma((2,))])(forward, result)
        return forward.reshape(start.shape), result.reshape(start.shape)

    return jax.shard_map(
        local,
        mesh=mesh,
        in_specs=(P("gx", "gy", None), P("gx", "gy", None), P("gx", "gy", None, None), P("gx", "gy", None, None),
                  P("gx", "gy", None, None), P(None, "gx", "gy", None, None)),
        out_specs=(P("gx", "gy", None), P("gx", "gy", None)),
        check_vma=False,
    )
```
